32 devices in a mesh: grp: 2 (over y), seq: 4 (over x, core), lab: 4 (over z).
Axes of the slice: x: 2, y: 2, z: 4, core: 2. Of those that a mesh axis runs over, the one named last changes fastest.
Arguments:
- hidden: bfloat16 [6144, 4096], P(('grp', 'seq'), 'lab'), parts along dimension 0, may hold values from -6 to 6
- proj_weight: bfloat16 [4096, 256], P('lab'), may hold values from -0.09375 to 0.09375
- queries: bfloat16 [9216, 256], P('lab'), may hold values from -0.25 to 0.25
- code_weight: bfloat16 [9216, 256], P('lab'), may hold values from -4 to 4
- code_bias: float32 [9216], P('lab'), may hold values from -0.5 to 0.5
- labels: int32 [4, 9216], P('grp', 'lab'), parts along dimension 0, may hold values 0 or 1
- code_counts: int32 [8, 9216], P(('grp', 'seq'), 'lab'), parts along dimension 0, may hold values from 0 to 119, as said below
Outputs:
- note_loss: float32 [4], P('grp'), parts along dimension 0
- grad_hidden: bfloat16 [6144, 4096], P(('grp', 'seq'), 'lab'), parts along dimension 0
- grad_proj: bfloat16 [8192, 256], P(('grp', 'lab', 'seq')), parts along dimension 0
- grad_queries: bfloat16 [18432, 256], P(('grp', 'lab', 'seq')), parts along dimension 0
- grad_code_weight: bfloat16 [18432, 256], P(('grp', 'lab', 'seq')), parts along dimension 0
- grad_bias: float32 [18432], P(('grp', 'lab')), parts along dimension 0
The draws below stay inside these ranges and needn't reach their ends.
There are 2 independent parts, one for each index of `grp`. The reference program is written for one: setup_inputs(seed, part) draws one part's arguments, and reference() takes and returns one part's arrays. A program takes and returns all parts, laid end to end along the dimension named above; an argument that names none is the same for every part. Nothing has to cross between parts.
Inputs may be any that keep to these rules, and one draw needn't show every extreme that they name: `code_counts`: entry (i, c) counts the occurrences of code c in the part of the training corpus read by loader i.
All inputs are finite; a program needn't handle non-finite values. No bound on the sum of `labels` on one device may be relied on, other than what follows from the above.
Results may differ from the reference program's by a relative error of at most 0.025.
Values may be sent and summed in bfloat16 or wider, within the bound.
A program may use at most 64 MiB of HBM per device.

```python
import math
import jax
import jax.numpy as jnp
from jax import lax

D = 4096
E = 256
C_DEV = 2304
TOK_DEV = 768
NOTES = 2
CODES = 9216
TOKENS = 3072
CNT_ROWS = 4
N_SEQ = 4
N_LAB = 4


def draw_code_counts(key, part):
    row_index = jnp.arange(CNT_ROWS, dtype=jnp.int32)[:, None]
    ceiling = 20 + 40 * row_index // (CNT_ROWS - 1) + jnp.zeros((CNT_ROWS, CODES), jnp.int32)
    drawn = jax.random.randint(key, (CNT_ROWS, CODES), 0, 2 * ceiling + 2, dtype=jnp.int32)
    return jnp.minimum(drawn, 119)


def set_ends(values, stream_key, least, high):
    longest = values.shape.index(max(values.shape))
    spots = []
    for shift in (0, 1):
        where = [jax.random.randint(jax.random.fold_in(stream_key, axis), (), 0, length) for axis, length in enumerate(values.shape)]
        where[longest] = (where[longest] + shift) % values.shape[longest]
        spots.append(tuple(where))
    return values.at[spots[0]].set(least).at[spots[1]].set(high)


def block_levels(own_key, dims, shards, least, high):
    factor_of = 1.0
    for axis_at, parts in shards:
        steps = jax.random.uniform(jax.random.fold_in(jax.random.fold_in(own_key, 6), axis_at), (parts,), jnp.float32, least / len(shards), high / len(shards))
        factor_of = factor_of * jnp.repeat(jnp.exp(steps), dims[axis_at] // parts).reshape((-1,) + (1,) * (len(dims) - 1 - axis_at))
    return factor_of


def gaussian(own_key, dims, deviation, bound, cuts=(), kind=jnp.bfloat16):
    result = jax.random.normal(own_key, dims, jnp.float32) * deviation
    if len(cuts) > 0:
        result = block_levels(own_key, dims, cuts, -0.22, 0.18) * result
    return jnp.clip(result, min=-bound, max=bound).astype(kind)


def setup_inputs(seed: int = 0, part: int = 0) -> dict:
    seeds = jax.random.split(jax.random.key(seed), 8)
    own_keys = jax.random.split(jax.random.fold_in(seeds[7], part), 8)
    return {
        "hidden": gaussian(own_keys[0], (TOKENS, D), 1.0, 6.0, ((0, 4), (1, 4))),
        "proj_weight": gaussian(seeds[1], (D, E), D ** -0.5, 0.09375, ((0, 4),)),
        "queries": jnp.clip(jax.random.uniform(seeds[2], (CODES, E), jnp.float32, -0.25, 0.25) * block_levels(seeds[2], (CODES, E), ((0, 4),), -0.4, 0.0), -0.25, 0.25).astype(jnp.bfloat16),
        "code_weight": gaussian(seeds[3], (CODES, E), 1.0, 4.0, ((0, 4),)),
        "code_bias": jnp.clip(jax.random.uniform(seeds[4], (CODES,), jnp.float32, -0.5, 0.5) * block_levels(seeds[4], (CODES,), ((0, 4),), -0.4, 0.0), -0.5, 0.5),
        "labels": set_ends((jax.random.randint(own_keys[5], (NOTES, CODES), 0, 16) < 1).astype(jnp.int32), jax.random.fold_in(own_keys[5], 1), 0, 1),
        "code_counts": draw_code_counts(jax.random.fold_in(jax.random.fold_in(seeds[7], part), 71), part),
    }


balance_beta = 0.9999
HIGH = lax.Precision.HIGHEST

def focal_loss(logit, target):
    prob = jax.nn.sigmoid(logit)
    return -(target * (1.0 - prob) * (1.0 - prob) * jax.nn.log_sigmoid(logit) + (1.0 - target) * prob * prob * jax.nn.log_sigmoid(-logit))

def rounded(value):
    return lax.optimization_barrier(value.astype(jnp.bfloat16)).astype(jnp.float32)

def to_blocks(table):
    return table.reshape(NOTES, N_LAB, C_DEV).transpose(1, 0, 2)

def reference(hidden, proj_weight, queries, code_weight, code_bias, labels, code_counts):
    pre = jnp.dot(hidden, proj_weight, preferred_element_type=jnp.float32)
    latent = jnp.tanh(pre).astype(jnp.bfloat16)
    latent_wide = latent.astype(jnp.float32)
    note_length = TOKENS // NOTES
    note_owner = jnp.arange(TOKENS, dtype=jnp.int32) // note_length
    member = (note_owner[None, :] == jnp.arange(NOTES, dtype=jnp.int32)[:, None]).astype(jnp.float32)
    query_blocks = queries.reshape(N_LAB, C_DEV, E)
    weight_blocks = code_weight.reshape(N_LAB, C_DEV, E)

    def attend(query_rows, weight_rows):
        scores = jnp.einsum('ce,te->ct', query_rows.astype(jnp.float32), latent_wide, precision=HIGH)
        values = jnp.einsum('ce,te->ct', weight_rows.astype(jnp.float32), latent_wide, precision=HIGH)
        return (jnp.exp(scores), values)

    def forward_block(block_pair):
        weights, values = attend(block_pair[0], block_pair[1])
        denominator = jnp.einsum('ct,nt->nc', weights, member, precision=HIGH)
        numerator = jnp.einsum('ct,nt->nc', weights * values, member, precision=HIGH)
        return (denominator, numerator)
    denominator_blocks, numerator_blocks = lax.map(forward_block, (query_blocks, weight_blocks))
    denominator = denominator_blocks.transpose(1, 0, 2).reshape(NOTES, CODES)
    numerator = numerator_blocks.transpose(1, 0, 2).reshape(NOTES, CODES)
    mean_value = numerator / denominator
    logits = mean_value + code_bias[None, :]
    occurrences = 1.0 + lax.optimization_barrier(jnp.sum(code_counts.astype(jnp.float32), 0))
    class_weight = (1.0 - balance_beta) / -jnp.expm1(occurrences * math.log(balance_beta))
    targets = labels.astype(jnp.float32)
    focal_value, pullback = jax.vjp(lambda point: focal_loss(point, targets), logits)
    focal_grad = pullback(jnp.ones_like(logits))[0]
    factor = CODES / jnp.sum(class_weight)
    note_loss = factor * lax.optimization_barrier(jnp.sum(focal_value * class_weight[None, :], 1))
    logit_grad = factor * class_weight[None, :] * focal_grad
    grad_bias = lax.optimization_barrier(jnp.sum(logit_grad, 0))

    def backward_block(total, blocks):
        query_rows, weight_rows, grad_rows, denom_rows, mean_rows = blocks
        weights, values = attend(query_rows, weight_rows)
        denom_tok = jnp.einsum('nc,nt->ct', denom_rows, member, precision=HIGH)
        grad_tok = jnp.einsum('nc,nt->ct', grad_rows, member, precision=HIGH)
        mean_tok = jnp.einsum('nc,nt->ct', mean_rows, member, precision=HIGH)
        value_part = weights / denom_tok * grad_tok
        score_part = value_part * (values - mean_tok)
        value_grad = rounded(value_part)
        score_grad = rounded(score_part)
        total = total + jnp.einsum('ct,ce->te', score_grad, query_rows.astype(jnp.float32), precision=HIGH)
        total = total + jnp.einsum('ct,ce->te', value_grad, weight_rows.astype(jnp.float32), precision=HIGH)
        latent_split = latent_wide.reshape(N_SEQ, TOK_DEV, E)
        query_terms = jnp.einsum('cst,ste->sce', score_grad.reshape(C_DEV, N_SEQ, TOK_DEV), latent_split, precision=HIGH)
        weight_terms = jnp.einsum('cst,ste->sce', value_grad.reshape(C_DEV, N_SEQ, TOK_DEV), latent_split, precision=HIGH)
        query_sum = lax.optimization_barrier(jnp.sum(rounded(query_terms), 0)).astype(jnp.bfloat16)
        weight_sum = lax.optimization_barrier(jnp.sum(rounded(weight_terms), 0)).astype(jnp.bfloat16)
        return (total, (query_sum, weight_sum))
    latent_grad, (query_parts, weight_parts) = lax.scan(backward_block, jnp.zeros((TOKENS, E), jnp.float32), (query_blocks, weight_blocks, to_blocks(logit_grad), to_blocks(denominator), to_blocks(mean_value)))
    grad_queries = query_parts.reshape(CODES, E)
    grad_code_weight = weight_parts.reshape(CODES, E)
    pre_grad = (latent_grad * (1.0 - latent_wide * latent_wide)).astype(jnp.bfloat16)
    grad_hidden = jnp.dot(pre_grad, proj_weight.T, preferred_element_type=jnp.float32).astype(jnp.bfloat16)
    hidden_wide = hidden.astype(jnp.float32).reshape(N_SEQ, TOK_DEV, D)
    pre_grad_wide = pre_grad.astype(jnp.float32).reshape(N_SEQ, TOK_DEV, E)
    proj_terms = jnp.einsum('std,ste->sde', hidden_wide, pre_grad_wide, precision=HIGH)
    grad_proj = lax.optimization_barrier(jnp.sum(rounded(proj_terms), 0)).astype(jnp.bfloat16)
    return (note_loss, grad_hidden, grad_proj, grad_queries, grad_code_weight, grad_bias)
```

```python
import functools
import math

import jax
import jax.numpy as jnp
from jax import lax
from jax.experimental import pallas as pl
from jax.experimental.pallas import tpu as pltpu
from jax.sharding import PartitionSpec as P

balance_beta = 0.9999
MESH = pl.DeviceIdType.MESH
F32 = jnp.float32
BF16 = jnp.bfloat16
CHUNK = 64
UNIT = 256
LAG_FWD = 6
LAG_BWD = 6


def expm1(x):
    series = jnp.ones_like(x)
    for order in range(10, 1, -1):
        series = 1.0 + x * series * (1.0 / order)
    return jnp.where(jnp.abs(x) < 0.5, x * series, jnp.exp(x) - 1.0)


def nt(a, b):
    return lax.dot_general(a, b, (((1,), (1,)), ((), ())), preferred_element_type=F32)


def tn(a, b):
    return lax.dot_general(a, b, (((0,), (0,)), ((), ())), preferred_element_type=F32)


def nn(a, b):
    return jnp.dot(a, b, preferred_element_type=F32)


def rows(start, size, multiple):
    return pl.ds(pl.multiple_of(start, multiple), size)


def fit(size, want):
    return want if size % want == 0 else size


def both_true(a, b):
    if isinstance(a, bool):
        return b if a else False
    if isinstance(b, bool):
        return a if b else False
    return jnp.logical_and(a, b)


def negate(a):
    return (not a) if isinstance(a, bool) else jnp.logical_not(a)


def when(condition, body):
    if isinstance(condition, bool):
        if condition:
            body()
    else:
        pl.when(condition)(body)


def far_first(count):
    return sorted(range(1, count), key=lambda d: -min(d, count - d))


def kernel(
    S, L, all_codes,
    hidden_h, proj_h, queries_h, codew_h, bias, labels, counts,
    loss_out, gh_out, gp_out, gq_out, gw_out, gb_out,
    hidden, proj, queries, codew, load_sem, own1, in1, lat, own2, in2, pg,
    w_s, v_s, tot, cnt, cw_sum, loss_s, cw_row, gd_row, mean_row, sg_s, vg_s,
    pq, pw, pp, q1, w1, p1, qs, ws, ps, q2, w2, p2,
    cnt_sem, tot_sem, cw_sem, loss_sem, up1_sem, down1_sem, up2_sem, down2_sem, st1_sem, st2_sem,
):
    T, D = hidden.shape
    C, E = queries.shape
    notes = labels.shape[0]
    X = S // 2
    per_note = S // notes
    unit = fit(T, UNIT)
    chunk = fit(unit, CHUNK)
    NC = T // chunk
    NU = T // unit
    per_unit = unit // chunk
    half = L // 2
    me_s = lax.axis_index("seq")
    me_l = lax.axis_index("lab")
    x = me_s // 2
    c = lax.rem(me_s, 2)
    lab_peers = [lax.rem(me_l + d, L) for d in range(1, L)]
    seq_peers = [lax.rem(me_s + d, S) for d in range(1, S)]
    side = me_l // half
    inward = me_l + 1 - 2 * side
    outward = lax.rem(me_l - 1 + 2 * side + L, L)
    if L == 2:
        inner, middle = False, True
    else:
        inner = jnp.logical_and(me_l != 0, me_l != L - 1)
        middle = jnp.logical_or(me_l == half - 1, me_l == half)
    across = 1 if L == 2 else jnp.where(middle, 1, 0)
    sent = []
    sent_if = []

    def remote(src, dst, send_sem, recv_sem, device):
        return pltpu.make_async_remote_copy(
            src_ref=src,
            dst_ref=dst,
            send_sem=send_sem,
            recv_sem=recv_sem,
            device_id=device,
            device_id_type=MESH,
        )

    def send(src, dst, sems, index, device):
        copy = remote(src, dst, sems.at[(0,) + index], sems.at[(1,) + index], device)
        copy.start()
        sent.append(copy)
        return copy

    barrier = pltpu.get_barrier_semaphore()
    for peer in lab_peers:
        pl.semaphore_signal(barrier, inc=1, device_id={"lab": peer}, device_id_type=MESH)
    for peer in seq_peers:
        pl.semaphore_signal(barrier, inc=1, device_id={"seq": peer}, device_id_type=MESH)

    loads = [
        pltpu.make_async_copy(src, dst, load_sem.at[k])
        for k, (src, dst) in enumerate(
            [(proj_h, proj), (hidden_h, hidden), (queries_h, queries), (codew_h, codew)]
        )
    ]
    for load in loads:
        load.start()
    cnt[me_s] = counts[...].astype(F32)

    def piece(k):
        if isinstance(k, int):
            return pl.ds(k * chunk, chunk)
        return rows(k * chunk, chunk, chunk)

    class Chain:
        def __init__(self, own, arrived, final, up, down, finish):
            self.own, self.arrived, self.final = own, arrived, final
            self.up, self.down, self.finish = up, down, finish

        def up_copy(self, k, slot):
            return remote(
                self.own.at[piece(k)], self.arrived.at[slot, piece(k)],
                self.up.at[2, k], self.up.at[slot, k], {"lab": inward},
            )

        def down_copy(self, k):
            at = self.final.at[piece(k)]
            return remote(at, at, self.down.at[0, k], self.down.at[1, k], {"lab": outward})

        def send_up(self, k):
            self.up_copy(k, across).start()

        def add_up(self, k):
            self.up_copy(k, 0).wait_recv()
            at = piece(k)
            total = self.own[at, :].astype(F32) + self.arrived[0, at, :].astype(F32)
            self.own[at, :] = total.astype(BF16)
            self.send_up(k)

        def settle(self, k, is_middle):
            def meet():
                self.up_copy(k, 1).wait_recv()
                at = piece(k)
                total = self.own[at, :].astype(F32) + self.arrived[1, at, :].astype(F32)
                self.final[at, :] = self.finish(total, at).astype(BF16)

            when(is_middle, meet)
            when(negate(is_middle), lambda: self.down_copy(k).wait_recv())

        def inner_steps(self, lag, beside):
            def body():
                for k in range(NC + lag):
                    if k < NC:
                        self.add_up(k)
                    if k >= lag:
                        self.settle(k - lag, True if L == 4 else middle)
                        self.down_copy(k - lag).start()

            when(inner, body)

        def outer_wait(self, first, count):
            def body():
                for i in range(count):
                    self.settle(first + i, L == 2)

            when(negate(inner), body)

        def drain(self):
            for k in range(NC):
                self.up_copy(k, 0).wait_send()

            def body():
                for k in range(NC):
                    self.down_copy(k).wait_send()

            when(inner, body)

    def finish_latent(total, at):
        return jnp.tanh(total)

    forward = Chain(own1, in1, lat, up1_sem, down1_sem, finish_latent)

    loads[0].wait()
    loads[1].wait()
    own1[...] = nn(hidden[...], proj[...]).astype(BF16)
    pl.semaphore_wait(barrier, S + L - 2)

    def start_forward():
        for k in range(NC):
            forward.send_up(k)

    when(negate(inner), start_forward)
    cnt_copies = [
        send(cnt.at[me_s], cnt.at[me_s], cnt_sem, (d,), {"seq": p})
        for d, p in enumerate(seq_peers)
    ]
    tot[me_s] = jnp.zeros((2, C), F32)
    loads[2].wait()
    loads[3].wait()
    for copy in cnt_copies:
        copy.wait_recv()
    occurrences = jnp.ones((1, C), F32)
    for s in range(S):
        occurrences = occurrences + cnt[s]
    class_weight = (1.0 - balance_beta) / -expm1(occurrences * math.log(balance_beta))
    cw_row[...] = class_weight
    cw_sum[me_l] = jnp.broadcast_to(jnp.sum(class_weight, 1, keepdims=True), (1, 128))
    cw_copies = [
        send(cw_sum.at[me_l], cw_sum.at[me_l], cw_sem, (d,), {"lab": p})
        for d, p in enumerate(lab_peers)
    ]

    forward.inner_steps(min(LAG_FWD, NC), None)

    @pl.loop(0, NU)
    def _(u):
        forward.outer_wait(u * per_unit, per_unit)
        at = rows(u * unit, unit, unit)
        block = lat[at, :]
        weights = jnp.exp(nt(block, queries[...]))
        values = nt(block, codew[...])
        w_s[at, :] = weights
        v_s[at, :] = values
        tot[me_s, 0:1, :] += jnp.sum(weights, 0, keepdims=True)
        tot[me_s, 1:2, :] += jnp.sum(weights * values, 0, keepdims=True)

    note = me_s // per_note
    sister_at = note * per_note

    def tot_copy(target, index):
        return remote(
            tot.at[me_s], tot.at[me_s], tot_sem.at[0, index], tot_sem.at[1, me_s],
            {"seq": target},
        )

    tot_sends = []
    for i in range(1, per_note):
        target = sister_at + lax.rem(me_s - sister_at + i, per_note)
        tot_sends.append(tot_copy(target, len(tot_sends)))
        tot_sends[-1].start()
    others = lax.rem(sister_at + per_note, S)
    for i in range(S - per_note):
        target = lax.rem(others + i, S)
        tot_sends.append(tot_copy(target, len(tot_sends)))
        tot_sends[-1].start()

    def tot_wait(source):
        remote(
            tot.at[source], tot.at[source], tot_sem.at[0, 0], tot_sem.at[1, source],
            {"seq": seq_peers[0]},
        ).wait_recv()

    for copy in cw_copies:
        copy.wait_recv()
    cw_total = cw_sum[0]
    for j in range(1, L):
        cw_total = cw_total + cw_sum[j]
    factor = all_codes / cw_total[0:1, 0:1]
    for i in range(1, per_note):
        tot_wait(sister_at + lax.rem(me_s - sister_at + i, per_note))

    def logits(n):
        both = tot[n * per_note]
        for i in range(1, per_note):
            both = both + tot[n * per_note + i]
        mean = both[1:2, :] / both[0:1, :]
        logit = mean + bias[...][None, :]
        y = labels[pl.ds(n, 1), :].astype(F32)
        t = jnp.exp(-jnp.abs(logit))
        l1p = jnp.log1p(t)
        big = 1.0 / (1.0 + t)
        small = t / (1.0 + t)
        p = jnp.where(logit >= 0, big, small)
        q = jnp.where(logit >= 0, small, big)
        ls_pos = jnp.minimum(logit, 0.0) - l1p
        ls_neg = jnp.minimum(-logit, 0.0) - l1p
        focal = -(y * q * q * ls_pos + (1.0 - y) * p * p * ls_neg)
        slope = -(
            y * q * q * (q - 2.0 * p * ls_pos)
            + (1.0 - y) * p * p * (2.0 * q * ls_neg - p)
        )
        return both[0:1, :], mean, focal, slope

    scaled = cw_row[...] * factor
    denominator, mean, _, slope = logits(note)
    gd_row[...] = scaled * slope / denominator
    mean_row[...] = mean

    def finish_grad(total, at):
        wide = lat[at, :].astype(F32)
        return total * (1.0 - wide * wide)

    backward = Chain(own2, in2, pg, up2_sem, down2_sem, finish_grad)

    @pl.loop(0, NU)
    def _(u):
        at = rows(u * unit, unit, unit)
        value_part = w_s[at, :] * gd_row[...]
        score_part = value_part * (v_s[at, :] - mean_row[...])
        vg = value_part.astype(BF16)
        sg = score_part.astype(BF16)
        vg_s[at, :] = vg
        sg_s[at, :] = sg
        own2[at, :] = (nn(sg, queries[...]) + nn(vg, codew[...])).astype(BF16)

        def start_unit():
            for i in range(per_unit):
                backward.send_up(u * per_unit + i)

        when(negate(inner), start_unit)

    sister = {"seq": x * 2 + (1 - c)}
    slots = list(range(1, X)) + [0]
    xs = [lax.rem(x + d, X) for d in range(X)]

    def block(ref, k):
        size = ref.shape[0] // S
        return rows(k * size, size, 16)

    def stage1_slot(a, part, first, d):
        k = xs[d] * 2 + (1 - c)
        return send(part.at[block(part, k)], first.at[d], st1_sem, (a, d), sister)

    def stage1(a, part, first):
        return {d: stage1_slot(a, part, first, d) for d in slots}

    def stage2(a, part, first, mid, second, arrived):
        out = []
        for d in range(1, X):
            arrived[d].wait_recv()
            mine = part[block(part, xs[d] * 2 + c), :].astype(F32)
            mid[d - 1] = (mine + first[d].astype(F32)).astype(BF16)
            out.append(
                send(
                    mid.at[d - 1], second.at[d - 1], st2_sem, (a, d - 1),
                    {"seq": xs[d] * 2 + c},
                )
            )
        return out

    def finish(part, first, second, arrived, copies, out):
        arrived[0].wait_recv()
        total = part[block(part, me_s), :].astype(F32) + first[0].astype(F32)
        for d, copy in enumerate(copies):
            copy.wait_recv()
            total = total + second[d].astype(F32)
        out[...] = total.astype(BF16)

    pw[...] = tn(vg_s[...], lat[...]).astype(BF16)
    w_first = stage1(1, pw, w1)
    pq[...] = tn(sg_s[...], lat[...]).astype(BF16)
    q_first = stage1(0, pq, q1)
    w_second = stage2(1, pw, w1, ws, w2, w_first)
    q_second = stage2(0, pq, q1, qs, q2, q_first)

    backward.inner_steps(min(LAG_BWD, NC), None)

    for i in range(S - per_note):
        tot_wait(lax.rem(others + i, S))
    bias_grad = jnp.zeros((1, C), F32)
    for n in range(notes):
        _, _, focal, slope = logits(n)
        bias_grad = bias_grad + scaled * slope
        loss_s[me_l, n : n + 1, :] = jnp.broadcast_to(
            jnp.sum(focal * cw_row[...], 1, keepdims=True), (1, 128)
        )
    gb_out[...] = bias_grad
    loss_copies = [
        send(loss_s.at[me_l], loss_s.at[me_l], loss_sem, (d,), {"lab": p})
        for d, p in enumerate(lab_peers)
    ]
    forward.drain()

    backward.outer_wait(0, NC)
    wide_block = 2 * (D // S)
    p_first = {}
    if wide_block % 128 == 0:
        for d in slots:
            at = rows(xs[d] * wide_block, wide_block, 128)
            pp[at, :] = tn(hidden[:, at], pg[...]).astype(BF16)
            p_first[d] = stage1_slot(2, pp, p1, d)
    else:
        pp[...] = tn(hidden[...], pg[...]).astype(BF16)
        p_first = stage1(2, pp, p1)
    p_second = stage2(2, pp, p1, ps, p2, p_first)
    gh_out[...] = nt(pg[...], proj[...]).astype(BF16)
    finish(pw, w1, w2, w_first, w_second, gw_out)
    finish(pq, q1, q2, q_first, q_second, gq_out)
    for copy in loss_copies:
        copy.wait_recv()
    loss = loss_s[0]
    for j in range(1, L):
        loss = loss + loss_s[j]
    loss_out[...] = loss * factor
    backward.drain()
    for copy in tot_sends:
        copy.wait_send()
    finish(pp, p1, p2, p_first, p_second, gp_out)
    for copy in sent:
        copy.wait_send()


def finish_kernel(loss, gh, gp, gq, gw, gb, loss_out, gh_out, gp_out, gq_out, gw_out, gb_out, sem):
    copies = []
    for k, (src, dst) in enumerate([(gh, gh_out), (gq, gq_out), (gw, gw_out), (gp, gp_out)]):
        copies.append(pltpu.make_async_copy(src, dst, sem.at[k]))
        copies[-1].start()
    gb_out[...] = gb[0, :]
    for n in range(loss_out.shape[0]):
        loss_out[n] = jnp.max(loss[n : n + 1, :])
    for copy in copies:
        copy.wait()


def per_device(hidden, proj_weight, queries, code_weight, code_bias, labels, code_counts):
    L = lax.axis_size("lab")
    S = lax.axis_size("seq")
    X = S // 2
    T, D = hidden.shape
    C, E = queries.shape
    notes = labels.shape[0]
    NC = T // fit(fit(T, UNIT), CHUNK)
    vmem = pltpu.VMEM
    dma = pltpu.SemaphoreType.DMA
    scratch = [
        vmem((T, D), BF16),
        vmem((D, E), BF16),
        vmem((C, E), BF16),
        vmem((C, E), BF16),
        dma((4,)),
        vmem((T, E), BF16),
        vmem((2, T, E), BF16),
        vmem((T, E), BF16),
        vmem((T, E), BF16),
        vmem((2, T, E), BF16),
        vmem((T, E), BF16),
        vmem((T, C), F32),
        vmem((T, C), F32),
        vmem((S, 2, C), F32),
        vmem((S, 1, C), F32),
        vmem((L, 1, 128), F32),
        vmem((L, notes, 128), F32),
        vmem((1, C), F32),
        vmem((1, C), F32),
        vmem((1, C), F32),
        vmem((T, C), BF16),
        vmem((T, C), BF16),
        vmem((C, E), BF16),
        vmem((C, E), BF16),
        vmem((D, E), BF16),
        vmem((X, C // S, E), BF16),
        vmem((X, C // S, E), BF16),
        vmem((X, D // S, E), BF16),
        vmem((X - 1, C // S, E), BF16),
        vmem((X - 1, C // S, E), BF16),
        vmem((X - 1, D // S, E), BF16),
        vmem((X - 1, C // S, E), BF16),
        vmem((X - 1, C // S, E), BF16),
        vmem((X - 1, D // S, E), BF16),
        dma((2, S - 1)),
        dma((2, S)),
        dma((2, L - 1)),
        dma((2, L - 1)),
        dma((3, NC)),
        dma((2, NC)),
        dma((3, NC)),
        dma((2, NC)),
        dma((2, 3, X)),
        dma((2, 3, X - 1)),
    ]
    whole = pl.BlockSpec(memory_space=pltpu.VMEM)
    anywhere = pl.BlockSpec(memory_space=pl.ANY)
    outs = pl.pallas_call(
        functools.partial(kernel, S, L, float(C * L)),
        out_shape=(
            pltpu.VMEM((notes, 128), F32),
            pltpu.VMEM((T, D), BF16),
            pltpu.VMEM((D // S, E), BF16),
            pltpu.VMEM((C // S, E), BF16),
            pltpu.VMEM((C // S, E), BF16),
            pltpu.VMEM((1, C), F32),
        ),
        in_specs=[anywhere] * 4 + [whole] * 3,
        scratch_shapes=scratch,
        compiler_params=pltpu.CompilerParams(
            collective_id=0, has_side_effects=True, vmem_limit_bytes=54 * 1024 * 1024
        ),
    )(hidden, proj_weight, queries, code_weight, code_bias, labels, code_counts)
    return pl.pallas_call(
        finish_kernel,
        out_shape=(
            jax.ShapeDtypeStruct((notes,), F32),
            jax.ShapeDtypeStruct((T, D), BF16),
            jax.ShapeDtypeStruct((D // S, E), BF16),
            jax.ShapeDtypeStruct((C // S, E), BF16),
            jax.ShapeDtypeStruct((C // S, E), BF16),
            jax.ShapeDtypeStruct((C,), F32),
        ),
        in_specs=[whole] * 6,
        out_specs=(
            pl.BlockSpec(memory_space=pltpu.SMEM),
            anywhere,
            anywhere,
            anywhere,
            anywhere,
            whole,
        ),
        scratch_shapes=[dma((4,))],
    )(*(pltpu.with_memory_space_constraint(out, pltpu.VMEM) for out in outs))


def solution(mesh):
    placed = (
        P(("grp", "seq"), "lab"),
        P("lab", None),
        P("lab", None),
        P("lab", None),
        P("lab"),
        P("grp", "lab"),
        P(("grp", "seq"), "lab"),
    )
    return jax.shard_map(
        per_device,
        mesh=mesh,
        in_specs=placed,
        out_specs=(
            P("grp"),
            P(("grp", "seq"), "lab"),
            P(("grp", "lab", "seq"), None),
            P(("grp", "lab", "seq"), None),
            P(("grp", "lab", "seq"), None),
            P(("grp", "lab")),
        ),
        check_vma=False,
    )
```

```python
import functools
import math

import jax
import jax.numpy as jnp
from jax import lax
from jax.experimental import pallas as pl
from jax.experimental.pallas import tpu as pltpu
from jax.sharding import PartitionSpec as P

balance_beta = 0.9999
MESH = pl.DeviceIdType.MESH
F32 = jnp.float32
BF16 = jnp.bfloat16
CHUNK = 64
UNIT = 256
LAG_FWD = 5
LAG_BWD = 5
MEET_W = 4
MEET_Q = 8


def expm1(x):
    series = jnp.ones_like(x)
    for order in range(10, 1, -1):
        series = 1.0 + x * series * (1.0 / order)
    return jnp.where(jnp.abs(x) < 0.5, x * series, jnp.exp(x) - 1.0)


def nt(a, b):
    return lax.dot_general(a, b, (((1,), (1,)), ((), ())), preferred_element_type=F32)


def tn(a, b):
    return lax.dot_general(a, b, (((0,), (0,)), ((), ())), preferred_element_type=F32)


def nn(a, b):
    return jnp.dot(a, b, preferred_element_type=F32)


def rows(start, size, multiple):
    return pl.ds(pl.multiple_of(start, multiple), size)


def fit(size, want):
    return want if size % want == 0 else size


def both_true(a, b):
    if isinstance(a, bool):
        return b if a else False
    if isinstance(b, bool):
        return a if b else False
    return jnp.logical_and(a, b)


def negate(a):
    return (not a) if isinstance(a, bool) else jnp.logical_not(a)


def when(condition, body):
    if isinstance(condition, bool):
        if condition:
            body()
    else:
        pl.when(condition)(body)


def far_first(count):
    return sorted(range(1, count), key=lambda d: -min(d, count - d))


def kernel(
    S, L, all_codes,
    hidden_h, proj_h, queries_h, codew_h, bias_h, labels_h, counts_h,
    loss_out, gh_out, gp_out, gq_out, gw_out, gb_out,
    hidden, proj, queries, codew, bias, labels, counts, load_sem, hidden_sem, own1, in1, lat, own2, in2, pg,
    w_s, v_s, tot, cnt, cw_sum, loss_s, cw_row, gd_row, mean_row, sg_s, vg_s,
    pq, pw, pp, pp32, q1, w1, p1, qs, ws, ps, q2, w2, p2,
    cnt_sem, tot_sem, cw_sem, loss_sem, up1_sem, down1_sem, up2_sem, down2_sem, st1_sem, st2_sem,
):
    T, D = hidden.shape
    C, E = queries.shape
    notes = labels.shape[0]
    X = S // 2
    per_note = S // notes
    unit = fit(T, UNIT)
    chunk = fit(unit, CHUNK)
    NC = T // chunk
    NU = T // unit
    per_unit = unit // chunk
    half = L // 2
    me_s = lax.axis_index("seq")
    me_l = lax.axis_index("lab")
    x = me_s // 2
    c = lax.rem(me_s, 2)
    lab_peers = [lax.rem(me_l + d, L) for d in range(1, L)]
    seq_peers = [lax.rem(me_s + d, S) for d in range(1, S)]
    side = me_l // half
    inward = me_l + 1 - 2 * side
    outward = lax.rem(me_l - 1 + 2 * side + L, L)
    if L == 2:
        inner, middle = False, True
    else:
        inner = jnp.logical_and(me_l != 0, me_l != L - 1)
        middle = jnp.logical_or(me_l == half - 1, me_l == half)
    across = 1 if L == 2 else jnp.where(middle, 1, 0)
    sent = []
    sent_if = []

    def remote(src, dst, send_sem, recv_sem, device):
        return pltpu.make_async_remote_copy(
            src_ref=src,
            dst_ref=dst,
            send_sem=send_sem,
            recv_sem=recv_sem,
            device_id=device,
            device_id_type=MESH,
        )

    def send(src, dst, sems, index, device):
        copy = remote(src, dst, sems.at[(0,) + index], sems.at[(1,) + index], device)
        copy.start()
        sent.append(copy)
        return copy

    barrier = pltpu.get_barrier_semaphore()
    for peer in lab_peers:
        pl.semaphore_signal(barrier, inc=1, device_id={"lab": peer}, device_id_type=MESH)
    for peer in seq_peers:
        pl.semaphore_signal(barrier, inc=1, device_id={"seq": peer}, device_id_type=MESH)

    def load(k, src, dst):
        copy = pltpu.make_async_copy(src, dst, load_sem.at[k])
        copy.start()
        return copy

    proj_load = load(0, proj_h, proj)
    hidden_loads = []
    for u in range(NU):
        at = pl.ds(u * unit, unit)
        hidden_loads.append(pltpu.make_async_copy(hidden_h.at[at], hidden.at[at], hidden_sem.at[u]))
        hidden_loads[-1].start()
    counts_load = load(1, counts_h, counts)
    bias_load = load(2, bias_h, bias)
    labels_load = load(3, labels_h, labels)

    def piece(k):
        if isinstance(k, int):
            return pl.ds(k * chunk, chunk)
        return rows(k * chunk, chunk, chunk)

    class Chain:
        def __init__(self, own, arrived, final, up, down, finish):
            self.own, self.arrived, self.final = own, arrived, final
            self.up, self.down, self.finish = up, down, finish

        def up_copy(self, k, slot):
            return remote(
                self.own.at[piece(k)], self.arrived.at[slot, piece(k)],
                self.up.at[2, k], self.up.at[slot, k], {"lab": inward},
            )

        def down_copy(self, k):
            at = self.final.at[piece(k)]
            return remote(at, at, self.down.at[0, k], self.down.at[1, k], {"lab": outward})

        def send_up(self, k):
            self.up_copy(k, across).start()

        def add_up(self, k):
            self.up_copy(k, 0).wait_recv()
            at = piece(k)
            total = self.own[at, :].astype(F32) + self.arrived[0, at, :].astype(F32)
            self.own[at, :] = total.astype(BF16)
            self.send_up(k)

        def settle(self, k, is_middle):
            def meet():
                self.up_copy(k, 1).wait_recv()
                at = piece(k)
                total = self.own[at, :].astype(F32) + self.arrived[1, at, :].astype(F32)
                self.final[at, :] = self.finish(total, at).astype(BF16)

            when(is_middle, meet)
            when(negate(is_middle), lambda: self.down_copy(k).wait_recv())

        def inner_steps(self, first, last, lag):
            def body():
                for k in range(first, last):
                    if k < NC:
                        self.add_up(k)
                    if k >= lag:
                        self.settle(k - lag, True if L == 4 else middle)
                        self.down_copy(k - lag).start()

            when(inner, body)

        def outer_wait(self, first, count):
            def body():
                for i in range(count):
                    self.settle(first + i, L == 2)

            when(negate(inner), body)

        def drain(self):
            for k in range(NC):
                self.up_copy(k, 0).wait_send()

            def body():
                for k in range(NC):
                    self.down_copy(k).wait_send()

            when(inner, body)

    def finish_latent(total, at):
        return jnp.tanh(total)

    forward = Chain(own1, in1, lat, up1_sem, down1_sem, finish_latent)

    proj_load.wait()
    for u in range(NU):
        hidden_loads[u].wait()
        at = pl.ds(u * unit, unit)
        own1[at, :] = nn(hidden[at, :], proj[...]).astype(BF16)
        if u == 0:
            pl.semaphore_wait(barrier, S + L - 2)

        def start_unit():
            for i in range(per_unit):
                forward.send_up(u * per_unit + i)

        when(negate(inner), start_unit)
    queries_load = load(4, queries_h, queries)
    codew_load = load(5, codew_h, codew)
    counts_load.wait()
    cnt[me_s] = counts[...].astype(F32)
    cnt_copies = [
        send(cnt.at[me_s], cnt.at[me_s], cnt_sem, (d,), {"seq": p})
        for d, p in enumerate(seq_peers)
    ]
    tot[me_s] = jnp.zeros((2, C), F32)
    for copy in cnt_copies:
        copy.wait_recv()
    occurrences = jnp.ones((1, C), F32)
    for s in range(S):
        occurrences = occurrences + cnt[s]
    class_weight = (1.0 - balance_beta) / -expm1(occurrences * math.log(balance_beta))
    cw_row[...] = class_weight
    cw_sum[me_l] = jnp.broadcast_to(jnp.sum(class_weight, 1, keepdims=True), (1, 128))
    cw_copies = [
        send(cw_sum.at[me_l], cw_sum.at[me_l], cw_sem, (d,), {"lab": p})
        for d, p in enumerate(lab_peers)
    ]

    lag = min(LAG_FWD, NC)
    forward.inner_steps(0, NC + lag, lag)
    queries_load.wait()
    codew_load.wait()

    @pl.loop(0, NU)
    def _(u):
        forward.outer_wait(u * per_unit, per_unit)
        at = rows(u * unit, unit, unit)
        block = lat[at, :]
        weights = jnp.exp(nt(block, queries[...]))
        values = nt(block, codew[...])
        w_s[at, :] = weights
        v_s[at, :] = values
        tot[me_s, 0:1, :] += jnp.sum(weights, 0, keepdims=True)
        tot[me_s, 1:2, :] += jnp.sum(weights * values, 0, keepdims=True)

    note = me_s // per_note
    sister_at = note * per_note

    def tot_copy(target, index):
        return remote(
            tot.at[me_s], tot.at[me_s], tot_sem.at[0, index], tot_sem.at[1, me_s],
            {"seq": target},
        )

    tot_sends = []
    for i in range(1, per_note):
        target = sister_at + lax.rem(me_s - sister_at + i, per_note)
        tot_sends.append(tot_copy(target, len(tot_sends)))
        tot_sends[-1].start()
    others = lax.rem(sister_at + per_note, S)
    for i in range(S - per_note):
        target = lax.rem(others + i, S)
        tot_sends.append(tot_copy(target, len(tot_sends)))
        tot_sends[-1].start()

    def tot_wait(source):
        remote(
            tot.at[source], tot.at[source], tot_sem.at[0, 0], tot_sem.at[1, source],
            {"seq": seq_peers[0]},
        ).wait_recv()

    for copy in cw_copies:
        copy.wait_recv()
    bias_load.wait()
    labels_load.wait()
    cw_total = cw_sum[0]
    for j in range(1, L):
        cw_total = cw_total + cw_sum[j]
    factor = all_codes / cw_total[0:1, 0:1]
    for i in range(1, per_note):
        tot_wait(sister_at + lax.rem(me_s - sister_at + i, per_note))

    def logits(n):
        both = tot[n * per_note]
        for i in range(1, per_note):
            both = both + tot[n * per_note + i]
        mean = both[1:2, :] / both[0:1, :]
        logit = mean + bias[...][None, :]
        y = labels[pl.ds(n, 1), :].astype(F32)
        t = jnp.exp(-jnp.abs(logit))
        l1p = jnp.log1p(t)
        big = 1.0 / (1.0 + t)
        small = t / (1.0 + t)
        p = jnp.where(logit >= 0, big, small)
        q = jnp.where(logit >= 0, small, big)
        ls_pos = jnp.minimum(logit, 0.0) - l1p
        ls_neg = jnp.minimum(-logit, 0.0) - l1p
        focal = -(y * q * q * ls_pos + (1.0 - y) * p * p * ls_neg)
        slope = -(
            y * q * q * (q - 2.0 * p * ls_pos)
            + (1.0 - y) * p * p * (2.0 * q * ls_neg - p)
        )
        return both[0:1, :], mean, focal, slope

    scaled = cw_row[...] * factor
    denominator, mean, _, slope = logits(note)
    gd_row[...] = scaled * slope / denominator
    mean_row[...] = mean

    def finish_grad(total, at):
        wide = lat[at, :].astype(F32)
        return total * (1.0 - wide * wide)

    backward = Chain(own2, in2, pg, up2_sem, down2_sem, finish_grad)

    @pl.loop(0, NU)
    def _(u):
        at = rows(u * unit, unit, unit)
        value_part = w_s[at, :] * gd_row[...]
        score_part = value_part * (v_s[at, :] - mean_row[...])
        vg = value_part.astype(BF16)
        sg = score_part.astype(BF16)
        vg_s[at, :] = vg
        sg_s[at, :] = sg
        own2[at, :] = (nn(sg, queries[...]) + nn(vg, codew[...])).astype(BF16)

        def start_unit():
            for i in range(per_unit):
                backward.send_up(u * per_unit + i)

        when(negate(inner), start_unit)

    sister = {"seq": x * 2 + (1 - c)}
    slots = list(range(1, X)) + [0]
    xs = [lax.rem(x + d, X) for d in range(X)]

    def block(ref, k):
        size = ref.shape[0] // S
        return rows(k * size, size, 16)

    def stage1_slot(a, part, first, d):
        k = xs[d] * 2 + (1 - c)
        return send(part.at[block(part, k)], first.at[d], st1_sem, (a, d), sister)

    def stage2(a, part, first, mid, second, arrived):
        out = []
        for d in range(1, X):
            arrived[d].wait_recv()
            mine = part[block(part, xs[d] * 2 + c), :].astype(F32)
            mid[d - 1] = (mine + first[d].astype(F32)).astype(BF16)
            out.append(
                send(
                    mid.at[d - 1], second.at[d - 1], st2_sem, (a, d - 1),
                    {"seq": xs[d] * 2 + c},
                )
            )
        return out

    def finish(part, first, second, arrived, copies, out):
        arrived[0].wait_recv()
        total = part[block(part, me_s), :].astype(F32) + first[0].astype(F32)
        for d, copy in enumerate(copies):
            copy.wait_recv()
            total = total + second[d].astype(F32)
        out[...] = total.astype(BF16)

    pw[...] = tn(vg_s[...], lat[...]).astype(BF16)
    w_first = {d: stage1_slot(1, pw, w1, d) for d in range(1, X)}
    pq[...] = tn(sg_s[...], lat[...]).astype(BF16)
    q_first = {d: stage1_slot(0, pq, q1, d) for d in range(1, X)}
    w_first[0] = stage1_slot(1, pw, w1, 0)
    q_first[0] = stage1_slot(0, pq, q1, 0)
    lag = min(LAG_BWD, NC)
    backward.inner_steps(0, MEET_W, lag)
    w_second = stage2(1, pw, w1, ws, w2, w_first)
    backward.inner_steps(MEET_W, MEET_Q, lag)
    q_second = stage2(0, pq, q1, qs, q2, q_first)
    backward.inner_steps(MEET_Q, NC + lag, lag)

    for i in range(S - per_note):
        tot_wait(lax.rem(others + i, S))
    bias_grad = jnp.zeros((1, C), F32)
    for n in range(notes):
        _, _, focal, slope = logits(n)
        bias_grad = bias_grad + scaled * slope
        loss_s[me_l, n : n + 1, :] = jnp.broadcast_to(
            jnp.sum(focal * cw_row[...], 1, keepdims=True), (1, 128)
        )
    gb_out[...] = bias_grad[0, :]
    loss_copies = [
        send(loss_s.at[me_l], loss_s.at[me_l], loss_sem, (d,), {"lab": p})
        for d, p in enumerate(lab_peers)
    ]
    forward.drain()

    early = (NU - 1) * unit
    wide_block = 2 * (D // S)
    by_slot = wide_block % 128 == 0
    if early:
        backward.outer_wait(0, early // chunk)
        pp32[...] = tn(hidden[0:early, :], pg[0:early, :])
    else:
        pp32[...] = jnp.zeros_like(pp32)
    backward.outer_wait(early // chunk, per_unit)
    p_first = {}
    if by_slot:
        for d in slots:
            at = rows(xs[d] * wide_block, wide_block, 128)
            pp[at, :] = (pp32[at, :] + tn(hidden[early:T, at], pg[early:T, :])).astype(BF16)
            p_first[d] = stage1_slot(2, pp, p1, d)
    else:
        pp[...] = (pp32[...] + tn(hidden[early:T, :], pg[early:T, :])).astype(BF16)
        p_first = {d: stage1_slot(2, pp, p1, d) for d in slots}
    p_second = stage2(2, pp, p1, ps, p2, p_first)
    gh_out[...] = nt(pg[...], proj[...]).astype(BF16)
    finish(pw, w1, w2, w_first, w_second, gw_out)
    finish(pq, q1, q2, q_first, q_second, gq_out)
    for copy in loss_copies:
        copy.wait_recv()
    loss = loss_s[0]
    for j in range(1, L):
        loss = loss + loss_s[j]
    loss_out[...] = loss * factor
    backward.drain()
    for copy in tot_sends:
        copy.wait_send()
    finish(pp, p1, p2, p_first, p_second, gp_out)
    for copy in sent:
        copy.wait_send()


def finish_kernel(
    loss, gh, gp, gq, gw, gb, loss_out, gh_out, gp_out, gq_out, gw_out, gb_out, loss_s, sem
):
    pairs = [(gh, gh_out), (gq, gq_out), (gw, gw_out), (gp, gp_out), (gb, gb_out), (loss_s, loss_out)]
    copies = [pltpu.make_async_copy(src, dst, sem.at[k]) for k, (src, dst) in enumerate(pairs)]
    for copy in copies[:-1]:
        copy.start()
    for n in range(loss_s.shape[0]):
        loss_s[n] = jnp.max(loss[n : n + 1, :])
    copies[-1].start()
    for copy in copies:
        copy.wait()


def per_device(hidden, proj_weight, queries, code_weight, code_bias, labels, code_counts):
    L = lax.axis_size("lab")
    S = lax.axis_size("seq")
    X = S // 2
    T, D = hidden.shape
    C, E = queries.shape
    notes = labels.shape[0]
    NU = T // fit(T, UNIT)
    NC = T // fit(fit(T, UNIT), CHUNK)
    vmem = pltpu.VMEM
    dma = pltpu.SemaphoreType.DMA
    scratch = [
        vmem((T, D), BF16),
        vmem((D, E), BF16),
        vmem((C, E), BF16),
        vmem((C, E), BF16),
        vmem((C,), F32),
        vmem((notes, C), jnp.int32),
        vmem((1, C), jnp.int32),
        dma((6,)),
        dma((NU,)),
        vmem((T, E), BF16),
        vmem((2, T, E), BF16),
        vmem((T, E), BF16),
        vmem((T, E), BF16),
        vmem((2, T, E), BF16),
        vmem((T, E), BF16),
        vmem((T, C), F32),
        vmem((T, C), F32),
        vmem((S, 2, C), F32),
        vmem((S, 1, C), F32),
        vmem((L, 1, 128), F32),
        vmem((L, notes, 128), F32),
        vmem((1, C), F32),
        vmem((1, C), F32),
        vmem((1, C), F32),
        vmem((T, C), BF16),
        vmem((T, C), BF16),
        vmem((C, E), BF16),
        vmem((C, E), BF16),
        vmem((D, E), BF16),
        vmem((D, E), F32),
        vmem((X, C // S, E), BF16),
        vmem((X, C // S, E), BF16),
        vmem((X, D // S, E), BF16),
        vmem((X - 1, C // S, E), BF16),
        vmem((X - 1, C // S, E), BF16),
        vmem((X - 1, D // S, E), BF16),
        vmem((X - 1, C // S, E), BF16),
        vmem((X - 1, C // S, E), BF16),
        vmem((X - 1, D // S, E), BF16),
        dma((2, S - 1)),
        dma((2, S)),
        dma((2, L - 1)),
        dma((2, L - 1)),
        dma((3, NC)),
        dma((2, NC)),
        dma((3, NC)),
        dma((2, NC)),
        dma((2, 3, X)),
        dma((2, 3, X - 1)),
    ]
    whole = pl.BlockSpec(memory_space=pltpu.VMEM)
    anywhere = pl.BlockSpec(memory_space=pl.ANY)
    outs = pl.pallas_call(
        functools.partial(kernel, S, L, float(C * L)),
        out_shape=(
            pltpu.VMEM((notes, 128), F32),
            pltpu.VMEM((T, D), BF16),
            pltpu.VMEM((D // S, E), BF16),
            pltpu.VMEM((C // S, E), BF16),
            pltpu.VMEM((C // S, E), BF16),
            pltpu.VMEM((C,), F32),
        ),
        in_specs=[anywhere] * 7,
        scratch_shapes=scratch,
        compiler_params=pltpu.CompilerParams(
            collective_id=0, has_side_effects=True, vmem_limit_bytes=54 * 1024 * 1024
        ),
    )(hidden, proj_weight, queries, code_weight, code_bias, labels, code_counts)
    return pl.pallas_call(
        finish_kernel,
        out_shape=(
            jax.ShapeDtypeStruct((notes,), F32),
            jax.ShapeDtypeStruct((T, D), BF16),
            jax.ShapeDtypeStruct((D // S, E), BF16),
            jax.ShapeDtypeStruct((C // S, E), BF16),
            jax.ShapeDtypeStruct((C // S, E), BF16),
            jax.ShapeDtypeStruct((C,), F32),
        ),
        in_specs=[whole] * 6,
        out_specs=(anywhere,) * 6,
        scratch_shapes=[pltpu.SMEM((notes,), F32), dma((6,))],
    )(*(pltpu.with_memory_space_constraint(out, pltpu.VMEM) for out in outs))


def solution(mesh):
    placed = (
        P(("grp", "seq"), "lab"),
        P("lab", None),
        P("lab", None),
        P("lab", None),
        P("lab"),
        P("grp", "lab"),
        P(("grp", "seq"), "lab"),
    )
    return jax.shard_map(
        per_device,
        mesh=mesh,
        in_specs=placed,
        out_specs=(
            P("grp"),
            P(("grp", "seq"), "lab"),
            P(("grp", "lab", "seq"), None),
            P(("grp", "lab", "seq"), None),
            P(("grp", "lab", "seq"), None),
            P(("grp", "lab")),
        ),
        check_vma=False,
    )
```

```python
import functools
import math

import jax
import jax.numpy as jnp
from jax import lax
from jax.experimental import pallas as pl
from jax.experimental.pallas import tpu as pltpu
from jax.sharding import PartitionSpec as P

balance_beta = 0.9999
MESH = pl.DeviceIdType.MESH
F32 = jnp.float32
BF16 = jnp.bfloat16
CHUNK = 64
UNIT = 256
LAGS_FWD = (5, 5)
LAGS_BWD = (5, 5)
TAIL = 2


def expm1(x):
    series = jnp.ones_like(x)
    for order in range(10, 1, -1):
        series = 1.0 + x * series * (1.0 / order)
    return jnp.where(jnp.abs(x) < 0.5, x * series, jnp.exp(x) - 1.0)


def nt(a, b):
    return lax.dot_general(a, b, (((1,), (1,)), ((), ())), preferred_element_type=F32)


def tn(a, b):
    return lax.dot_general(a, b, (((0,), (0,)), ((), ())), preferred_element_type=F32)


def nn(a, b):
    return jnp.dot(a, b, preferred_element_type=F32)


def rows(start, size, multiple):
    return pl.ds(pl.multiple_of(start, multiple), size)


def fit(size, want):
    return want if size % want == 0 else size


def both_true(a, b):
    if isinstance(a, bool):
        return b if a else False
    if isinstance(b, bool):
        return a if b else False
    return jnp.logical_and(a, b)


def negate(a):
    return (not a) if isinstance(a, bool) else jnp.logical_not(a)


def when(condition, body):
    if isinstance(condition, bool):
        if condition:
            body()
    else:
        pl.when(condition)(body)


def far_first(count):
    return sorted(range(1, count), key=lambda d: -min(d, count - d))


def kernel(
    S, L, all_codes,
    hidden_h, proj_h, queries_h, codew_h, bias_h, labels_h, counts_h,
    loss_out, gh_out, gp_out, gq_out, gw_out, gb_out,
    hidden, proj, queries, codew, bias, labels, counts, load_sem, hidden_sem, own1, in1, lat, own2, in2, pg,
    w_s, v_s, tot, cnt, cw_sum, loss_s, cw_row, gd_row, mean_row, sg_s, vg_s,
    pq, pw, pp, pp32, q1, w1, p1, qs, ws, ps, q2, w2, p2,
    cnt_sem, tot_sem, cw_sem, loss_sem, up1_sem, down1_sem, direct1_sem, up2_sem, down2_sem, direct2_sem, st1_sem, st2_sem,
):
    T, D = hidden.shape
    C, E = queries.shape
    notes = labels.shape[0]
    X = S // 2
    per_note = S // notes
    unit = fit(T, UNIT)
    chunk = fit(unit, CHUNK)
    NC = T // chunk
    NU = T // unit
    per_unit = unit // chunk
    tail = TAIL if L == 4 else 0
    NT = NC - tail
    half = L // 2
    me_s = lax.axis_index("seq")
    me_l = lax.axis_index("lab")
    x = me_s // 2
    c = lax.rem(me_s, 2)
    lab_peers = [lax.rem(me_l + d, L) for d in range(1, L)]
    seq_peers = [lax.rem(me_s + d, S) for d in range(1, S)]
    side = me_l // half
    inward = me_l + 1 - 2 * side
    outward = lax.rem(me_l - 1 + 2 * side + L, L)
    if L == 2:
        inner, middle = False, True
    else:
        inner = jnp.logical_and(me_l != 0, me_l != L - 1)
        middle = jnp.logical_or(me_l == half - 1, me_l == half)
    across = 1 if L == 2 else jnp.where(middle, 1, 0)
    sent = []
    sent_if = []

    def remote(src, dst, send_sem, recv_sem, device):
        return pltpu.make_async_remote_copy(
            src_ref=src,
            dst_ref=dst,
            send_sem=send_sem,
            recv_sem=recv_sem,
            device_id=device,
            device_id_type=MESH,
        )

    def send(src, dst, sems, index, device):
        copy = remote(src, dst, sems.at[(0,) + index], sems.at[(1,) + index], device)
        copy.start()
        sent.append(copy)
        return copy

    barrier = pltpu.get_barrier_semaphore()
    far = lax.rem(me_l + 2, L)

    def greet(peer):
        pl.semaphore_signal(barrier, inc=1, device_id={"lab": peer}, device_id_type=MESH)

    greet(inward)
    when(inner, lambda: greet(outward))
    if tail:
        greet(far)
    greetings = S + (1 if tail else 0) + (0 if L == 2 else jnp.where(inner, 1, 0))

    for peer in seq_peers:
        pl.semaphore_signal(barrier, inc=1, device_id={"seq": peer}, device_id_type=MESH)

    def load(k, src, dst):
        copy = pltpu.make_async_copy(src, dst, load_sem.at[k])
        copy.start()
        return copy

    proj_load = load(0, proj_h, proj)
    hidden_loads = []
    for u in range(NU):
        at = pl.ds(u * unit, unit)
        hidden_loads.append(pltpu.make_async_copy(hidden_h.at[at], hidden.at[at], hidden_sem.at[u]))
        hidden_loads[-1].start()
    counts_load = load(1, counts_h, counts)
    bias_load = load(2, bias_h, bias)
    labels_load = load(3, labels_h, labels)

    def piece(k):
        if isinstance(k, int):
            return pl.ds(k * chunk, chunk)
        return rows(k * chunk, chunk, chunk)

    class Chain:
        def __init__(self, own, arrived, final, up, down, direct, finish):
            self.own, self.arrived, self.final = own, arrived, final
            self.up, self.down, self.direct, self.finish = up, down, direct, finish

        def up_copy(self, k, slot):
            return remote(
                self.own.at[piece(k)], self.arrived.at[slot, piece(k)],
                self.up.at[2, k], self.up.at[slot, k], {"lab": inward},
            )

        def down_copy(self, k):
            at = self.final.at[piece(k)]
            return remote(at, at, self.down.at[0, k], self.down.at[1, k], {"lab": outward})

        def direct_copy(self, k):
            return remote(
                self.own.at[piece(k)], self.arrived.at[2, piece(k)],
                self.direct.at[0, k - NT], self.direct.at[1, k - NT], {"lab": far},
            )

        def send_up(self, k):
            self.up_copy(k, across).start()

        def start_unit(self, u):
            chunks = range(u * per_unit, (u + 1) * per_unit)

            def from_outer():
                for k in chunks:
                    if k < NT:
                        self.send_up(k)
                for k in chunks:
                    if k >= NT:
                        self.direct_copy(k).start()
                        self.send_up(k)

            def from_inner():
                for k in chunks:
                    if k >= NT:
                        self.send_up(k)

            when(negate(inner), from_outer)
            if chunks[-1] >= NT:
                when(inner, from_inner)

        def sum_of(self, at, slots):
            return sum(self.arrived[slot, at, :].astype(F32) for slot in slots)

        def add_up(self, k):
            self.up_copy(k, 0).wait_recv()
            at = piece(k)
            self.own[at, :] = (self.own[at, :].astype(F32) + self.sum_of(at, [0])).astype(BF16)
            self.send_up(k)

        def settle(self, k, is_middle):
            def meet():
                self.up_copy(k, 1).wait_recv()
                at = piece(k)
                total = self.own[at, :].astype(F32) + self.sum_of(at, [1])
                self.final[at, :] = self.finish(total, at).astype(BF16)

            when(is_middle, meet)
            when(negate(is_middle), lambda: self.down_copy(k).wait_recv())

        def settle_direct(self, k):
            self.up_copy(k, 1).wait_recv()
            self.up_copy(k, 0).wait_recv()
            self.direct_copy(k).wait_recv()
            at = piece(k)
            near = self.own[at, :].astype(F32) + self.sum_of(at, [0])
            total = near + self.sum_of(at, [1, 2])
            self.final[at, :] = self.finish(total, at).astype(BF16)

        def inner_steps(self, lags):
            def steps(lag):
                for k in range(NT + lag):
                    if k < NT:
                        self.add_up(k)
                    if k >= lag:
                        self.settle(k - lag, True if L == 4 else middle)
                        self.down_copy(k - lag).start()
                for k in range(NT, NC):
                    self.settle_direct(k)
                    self.down_copy(k).start()

            def body():
                if lags[0] == lags[1]:
                    steps(lags[0])
                else:
                    pl.when(c == 0)(lambda: steps(lags[0]))
                    pl.when(c == 1)(lambda: steps(lags[1]))

            when(inner, body)

        def outer_wait(self, first, count):
            def body():
                for i in range(count):
                    self.settle(first + i, L == 2)

            when(negate(inner), body)

        def drain(self):
            for k in range(NC):
                self.up_copy(k, 0).wait_send()

            def from_inner():
                for k in range(NC):
                    self.down_copy(k).wait_send()

            def from_outer():
                for k in range(NT, NC):
                    self.direct_copy(k).wait_send()

            when(inner, from_inner)
            if tail:
                when(negate(inner), from_outer)

    def finish_latent(total, at):
        return jnp.tanh(total)

    forward = Chain(own1, in1, lat, up1_sem, down1_sem, direct1_sem, finish_latent)

    proj_load.wait()
    for u in range(NU):
        hidden_loads[u].wait()
        at = pl.ds(u * unit, unit)
        own1[at, :] = nn(hidden[at, :], proj[...]).astype(BF16)
        if u == 0:
            pl.semaphore_wait(barrier, greetings)
        forward.start_unit(u)
    queries_load = load(4, queries_h, queries)
    codew_load = load(5, codew_h, codew)
    counts_load.wait()
    cnt[me_s] = counts[...].astype(F32)
    cnt_copies = [
        send(cnt.at[me_s], cnt.at[me_s], cnt_sem, (d,), {"seq": p})
        for d, p in enumerate(seq_peers)
    ]
    tot[me_s] = jnp.zeros((2, C), F32)
    forward.inner_steps(LAGS_FWD)
    for copy in cnt_copies:
        copy.wait_recv()
    occurrences = jnp.ones((1, C), F32)
    for s in range(S):
        occurrences = occurrences + cnt[s]
    class_weight = (1.0 - balance_beta) / -expm1(occurrences * math.log(balance_beta))
    cw_row[...] = class_weight
    cw_sum[me_l] = jnp.broadcast_to(jnp.sum(class_weight, 1, keepdims=True), (1, 128))
    queries_load.wait()
    codew_load.wait()

    @pl.loop(0, NU)
    def _(u):
        forward.outer_wait(u * per_unit, per_unit)
        at = rows(u * unit, unit, unit)
        block = lat[at, :]
        weights = jnp.exp(nt(block, queries[...]))
        values = nt(block, codew[...])
        w_s[at, :] = weights
        v_s[at, :] = values
        tot[me_s, 0:1, :] += jnp.sum(weights, 0, keepdims=True)
        tot[me_s, 1:2, :] += jnp.sum(weights * values, 0, keepdims=True)

    note = me_s // per_note
    sister_at = note * per_note

    def tot_copy(target, index):
        return remote(
            tot.at[me_s], tot.at[me_s], tot_sem.at[0, index], tot_sem.at[1, me_s],
            {"seq": target},
        )

    tot_sends = []
    for i in range(1, per_note):
        target = sister_at + lax.rem(me_s - sister_at + i, per_note)
        tot_sends.append(tot_copy(target, len(tot_sends)))
        tot_sends[-1].start()
    others = lax.rem(sister_at + per_note, S)
    for i in range(S - per_note):
        target = lax.rem(others + i, S)
        tot_sends.append(tot_copy(target, len(tot_sends)))
        tot_sends[-1].start()

    def tot_wait(source):
        remote(
            tot.at[source], tot.at[source], tot_sem.at[0, 0], tot_sem.at[1, source],
            {"seq": seq_peers[0]},
        ).wait_recv()

    cw_copies = [
        send(cw_sum.at[me_l], cw_sum.at[me_l], cw_sem, (d,), {"lab": p})
        for d, p in enumerate(lab_peers)
    ]

    bias_load.wait()
    labels_load.wait()
    for i in range(1, per_note):
        tot_wait(sister_at + lax.rem(me_s - sister_at + i, per_note))

    def logits(n):
        both = tot[n * per_note]
        for i in range(1, per_note):
            both = both + tot[n * per_note + i]
        mean = both[1:2, :] / both[0:1, :]
        logit = mean + bias[...][None, :]
        y = labels[pl.ds(n, 1), :].astype(F32)
        t = jnp.exp(-jnp.abs(logit))
        l1p = jnp.log1p(t)
        big = 1.0 / (1.0 + t)
        small = t / (1.0 + t)
        p = jnp.where(logit >= 0, big, small)
        q = jnp.where(logit >= 0, small, big)
        ls_pos = jnp.minimum(logit, 0.0) - l1p
        ls_neg = jnp.minimum(-logit, 0.0) - l1p
        focal = -(y * q * q * ls_pos + (1.0 - y) * p * p * ls_neg)
        slope = -(
            y * q * q * (q - 2.0 * p * ls_pos)
            + (1.0 - y) * p * p * (2.0 * q * ls_neg - p)
        )
        return both[0:1, :], mean, focal, slope

    denominator, mean, _, slope = logits(note)
    gd_row[...] = cw_row[...] * slope / denominator
    mean_row[...] = mean

    def finish_grad(total, at):
        wide = lat[at, :].astype(F32)
        return total * factor * (1.0 - wide * wide)

    sister = {"seq": x * 2 + (1 - c)}
    slots = list(range(1, X)) + [0]
    xs = [lax.rem(x + d, X) for d in range(X)]

    def block(ref, k):
        size = ref.shape[0] // S
        return rows(k * size, size, 16)

    def stage1_slot(a, part, first, d):
        k = xs[d] * 2 + (1 - c)
        return send(part.at[block(part, k)], first.at[d], st1_sem, (a, d), sister)

    def stage2(a, part, first, mid, second, arrived):
        out = []
        for d in range(1, X):
            arrived[d].wait_recv()
            mine = part[block(part, xs[d] * 2 + c), :].astype(F32)
            mid[d - 1] = (mine + first[d].astype(F32)).astype(BF16)
            out.append(
                send(
                    mid.at[d - 1], second.at[d - 1], st2_sem, (a, d - 1),
                    {"seq": xs[d] * 2 + c},
                )
            )
        return out

    def finish(part, first, second, arrived, copies, scale, out):
        arrived[0].wait_recv()
        total = part[block(part, me_s), :].astype(F32) + first[0].astype(F32)
        for d, copy in enumerate(copies):
            copy.wait_recv()
            total = total + second[d].astype(F32)
        out[...] = (total * scale).astype(BF16)

    backward = Chain(own2, in2, pg, up2_sem, down2_sem, direct2_sem, finish_grad)

    def parts(u):
        at = pl.ds(u * unit, unit)
        value_part = w_s[at, :] * gd_row[...]
        vg_s[at, :] = value_part.astype(BF16)
        sg_s[at, :] = (value_part * (v_s[at, :] - mean_row[...])).astype(BF16)

    def latent_unit(u):
        at = pl.ds(u * unit, unit)
        total = nn(sg_s[at, :], queries[...]) + nn(vg_s[at, :], codew[...])
        own2[at, :] = total.astype(BF16)
        backward.start_unit(u)

    code_block = 2 * (C // S)
    code_by_slot = code_block % 128 == 0

    def code_part(grads, part, d):
        at = rows(xs[d] * code_block, code_block, 128 if code_by_slot else 16)
        if code_by_slot:
            part[at, :] = tn(grads[:, at], lat[...]).astype(BF16)
        elif d == slots[0]:
            part[...] = tn(grads[...], lat[...]).astype(BF16)

    parts(0)
    latent_unit(0)
    for u in range(1, NU):
        parts(u)
    w_first, q_first = {}, {}
    for d in range(1, X):
        code_part(vg_s, pw, d)
        w_first[d] = stage1_slot(1, pw, w1, d)
    for u in range(1, min(2, NU)):
        latent_unit(u)
    for d in range(1, X):
        code_part(sg_s, pq, d)
        q_first[d] = stage1_slot(0, pq, q1, d)
    for u in range(2, NU):
        latent_unit(u)
    w_second = stage2(1, pw, w1, ws, w2, w_first)
    code_part(vg_s, pw, 0)
    w_first[0] = stage1_slot(1, pw, w1, 0)
    code_part(sg_s, pq, 0)
    q_first[0] = stage1_slot(0, pq, q1, 0)
    q_second = stage2(0, pq, q1, qs, q2, q_first)
    for copy in cw_copies:
        copy.wait_recv()
    cw_total = cw_sum[0]
    for j in range(1, L):
        cw_total = cw_total + cw_sum[j]
    factor = all_codes / cw_total[0:1, 0:1]
    backward.inner_steps(LAGS_BWD)

    for i in range(S - per_note):
        tot_wait(lax.rem(others + i, S))
    bias_grad = jnp.zeros((1, C), F32)
    for n in range(notes):
        _, _, focal, slope = logits(n)
        bias_grad = bias_grad + cw_row[...] * slope
        loss_s[me_l, n : n + 1, :] = jnp.broadcast_to(
            jnp.sum(focal * cw_row[...], 1, keepdims=True), (1, 128)
        )
    gb_out[...] = (bias_grad * factor)[0, :]
    loss_copies = [
        send(loss_s.at[me_l], loss_s.at[me_l], loss_sem, (d,), {"lab": p})
        for d, p in enumerate(lab_peers)
    ]
    forward.drain()

    early = (NU - 1) * unit
    wide_block = 2 * (D // S)
    by_slot = wide_block % 128 == 0
    if early:
        backward.outer_wait(0, early // chunk)
        pp32[...] = tn(hidden[0:early, :], pg[0:early, :])
    else:
        pp32[...] = jnp.zeros_like(pp32)
    backward.outer_wait(early // chunk, per_unit)
    p_first = {}
    if by_slot:
        for d in slots:
            at = rows(xs[d] * wide_block, wide_block, 128)
            pp[at, :] = (pp32[at, :] + tn(hidden[early:T, at], pg[early:T, :])).astype(BF16)
            p_first[d] = stage1_slot(2, pp, p1, d)
    else:
        pp[...] = (pp32[...] + tn(hidden[early:T, :], pg[early:T, :])).astype(BF16)
        p_first = {d: stage1_slot(2, pp, p1, d) for d in slots}
    p_second = stage2(2, pp, p1, ps, p2, p_first)
    gh_out[...] = nt(pg[...], proj[...]).astype(BF16)
    finish(pw, w1, w2, w_first, w_second, factor, gw_out)
    finish(pq, q1, q2, q_first, q_second, factor, gq_out)
    for copy in loss_copies:
        copy.wait_recv()
    loss = loss_s[0]
    for j in range(1, L):
        loss = loss + loss_s[j]
    loss_out[...] = loss * factor
    backward.drain()
    for copy in tot_sends:
        copy.wait_send()
    finish(pp, p1, p2, p_first, p_second, 1.0, gp_out)
    for copy in sent:
        copy.wait_send()


def finish_kernel(
    loss, gh, gp, gq, gw, gb, loss_out, gh_out, gp_out, gq_out, gw_out, gb_out, loss_s, sem
):
    pairs = [(gh, gh_out), (gq, gq_out), (gw, gw_out), (gp, gp_out), (gb, gb_out), (loss_s, loss_out)]
    copies = [pltpu.make_async_copy(src, dst, sem.at[k]) for k, (src, dst) in enumerate(pairs)]
    for copy in copies[:-1]:
        copy.start()
    for n in range(loss_s.shape[0]):
        loss_s[n] = jnp.max(loss[n : n + 1, :])
    copies[-1].start()
    for copy in copies:
        copy.wait()


def per_device(hidden, proj_weight, queries, code_weight, code_bias, labels, code_counts):
    L = lax.axis_size("lab")
    S = lax.axis_size("seq")
    X = S // 2
    T, D = hidden.shape
    C, E = queries.shape
    notes = labels.shape[0]
    NU = T // fit(T, UNIT)
    NC = T // fit(fit(T, UNIT), CHUNK)
    vmem = pltpu.VMEM
    dma = pltpu.SemaphoreType.DMA
    scratch = [
        vmem((T, D), BF16),
        vmem((D, E), BF16),
        vmem((C, E), BF16),
        vmem((C, E), BF16),
        vmem((C,), F32),
        vmem((notes, C), jnp.int32),
        vmem((1, C), jnp.int32),
        dma((6,)),
        dma((NU,)),
        vmem((T, E), BF16),
        vmem((3, T, E), BF16),
        vmem((T, E), BF16),
        vmem((T, E), BF16),
        vmem((3, T, E), BF16),
        vmem((T, E), BF16),
        vmem((T, C), F32),
        vmem((T, C), F32),
        vmem((S, 2, C), F32),
        vmem((S, 1, C), F32),
        vmem((L, 1, 128), F32),
        vmem((L, notes, 128), F32),
        vmem((1, C), F32),
        vmem((1, C), F32),
        vmem((1, C), F32),
        vmem((T, C), BF16),
        vmem((T, C), BF16),
        vmem((C, E), BF16),
        vmem((C, E), BF16),
        vmem((D, E), BF16),
        vmem((D, E), F32),
        vmem((X, C // S, E), BF16),
        vmem((X, C // S, E), BF16),
        vmem((X, D // S, E), BF16),
        vmem((X - 1, C // S, E), BF16),
        vmem((X - 1, C // S, E), BF16),
        vmem((X - 1, D // S, E), BF16),
        vmem((X - 1, C // S, E), BF16),
        vmem((X - 1, C // S, E), BF16),
        vmem((X - 1, D // S, E), BF16),
        dma((2, S - 1)),
        dma((2, S)),
        dma((2, L - 1)),
        dma((2, L - 1)),
        dma((3, NC)),
        dma((2, NC)),
        dma((2, TAIL)),
        dma((3, NC)),
        dma((2, NC)),
        dma((2, TAIL)),
        dma((2, 3, X)),
        dma((2, 3, X - 1)),
    ]
    whole = pl.BlockSpec(memory_space=pltpu.VMEM)
    anywhere = pl.BlockSpec(memory_space=pl.ANY)
    outs = pl.pallas_call(
        functools.partial(kernel, S, L, float(C * L)),
        out_shape=(
            pltpu.VMEM((notes, 128), F32),
            pltpu.VMEM((T, D), BF16),
            pltpu.VMEM((D // S, E), BF16),
            pltpu.VMEM((C // S, E), BF16),
            pltpu.VMEM((C // S, E), BF16),
            pltpu.VMEM((C,), F32),
        ),
        in_specs=[anywhere] * 7,
        scratch_shapes=scratch,
        compiler_params=pltpu.CompilerParams(
            collective_id=0, has_side_effects=True, vmem_limit_bytes=54 * 1024 * 1024
        ),
    )(hidden, proj_weight, queries, code_weight, code_bias, labels, code_counts)
    return pl.pallas_call(
        finish_kernel,
        out_shape=(
            jax.ShapeDtypeStruct((notes,), F32),
            jax.ShapeDtypeStruct((T, D), BF16),
            jax.ShapeDtypeStruct((D // S, E), BF16),
            jax.ShapeDtypeStruct((C // S, E), BF16),
            jax.ShapeDtypeStruct((C // S, E), BF16),
            jax.ShapeDtypeStruct((C,), F32),
        ),
        in_specs=[whole] * 6,
        out_specs=(anywhere,) * 6,
        scratch_shapes=[pltpu.SMEM((notes,), F32), dma((6,))],
    )(*(pltpu.with_memory_space_constraint(out, pltpu.VMEM) for out in outs))


def solution(mesh):
    placed = (
        P(("grp", "seq"), "lab"),
        P("lab", None),
        P("lab", None),
        P("lab", None),
        P("lab"),
        P("grp", "lab"),
        P(("grp", "seq"), "lab"),
    )
    return jax.shard_map(
        per_device,
        mesh=mesh,
        in_specs=placed,
        out_specs=(
            P("grp"),
            P(("grp", "seq"), "lab"),
            P(("grp", "lab", "seq"), None),
            P(("grp", "lab", "seq"), None),
            P(("grp", "lab", "seq"), None),
            P(("grp", "lab")),
        ),
        check_vma=False,
    )
```

```python
import functools
import math

import jax
import jax.numpy as jnp
from jax import lax
from jax.experimental import pallas as pl
from jax.experimental.pallas import tpu as pltpu
from jax.sharding import PartitionSpec as P

balance_beta = 0.9999
MESH = pl.DeviceIdType.MESH
F32 = jnp.float32
BF16 = jnp.bfloat16
CHUNK = 64
UNIT = 256
LAG_FWD = 5
LAG_BWD = 5
MEET_W = 3
MEET_Q = 12
Q_PARTS = 3
Q_AT = (1, 4, 6, 7)


def expm1(x):
    series = jnp.ones_like(x)
    for order in range(10, 1, -1):
        series = 1.0 + x * series * (1.0 / order)
    return jnp.where(jnp.abs(x) < 0.5, x * series, jnp.exp(x) - 1.0)


def nt(a, b):
    return lax.dot_general(a, b, (((1,), (1,)), ((), ())), preferred_element_type=F32)


def tn(a, b):
    return lax.dot_general(a, b, (((0,), (0,)), ((), ())), preferred_element_type=F32)


def nn(a, b):
    return jnp.dot(a, b, preferred_element_type=F32)


def rows(start, size, multiple):
    return pl.ds(pl.multiple_of(start, multiple), size)


def fit(size, want):
    return want if size % want == 0 else size


def both_true(a, b):
    if isinstance(a, bool):
        return b if a else False
    if isinstance(b, bool):
        return a if b else False
    return jnp.logical_and(a, b)


def negate(a):
    return (not a) if isinstance(a, bool) else jnp.logical_not(a)


def when(condition, body):
    if isinstance(condition, bool):
        if condition:
            body()
    else:
        pl.when(condition)(body)


def far_first(count):
    return sorted(range(1, count), key=lambda d: -min(d, count - d))


def kernel(
    S, L, all_codes,
    hidden_h, proj_h, queries_h, codew_h, bias_h, labels_h, counts_h,
    loss_out, gh_out, gp_out, gq_out, gw_out, gb_out,
    hidden, proj, queries, codew, bias, labels, counts, load_sem, hidden_sem, own1, in1, lat, own2, in2, pg,
    w_s, v_s, tot, cnt, cw_sum, loss_s, cw_row, gd_row, mean_row, sg_s, vg_s,
    pq, pw, pp, pp32, q1, w1, p1, qs, ws, ps, q2, w2, p2,
    cnt_sem, tot_sem, cw_sem, loss_sem, up1_sem, down1_sem, up2_sem, down2_sem, st1_sem, st2_sem,
):
    T, D = hidden.shape
    C, E = queries.shape
    notes = labels.shape[0]
    X = S // 2
    per_note = S // notes
    unit = fit(T, UNIT)
    chunk = fit(unit, CHUNK)
    NC = T // chunk
    NU = T // unit
    per_unit = unit // chunk
    half = L // 2
    me_s = lax.axis_index("seq")
    me_l = lax.axis_index("lab")
    x = me_s // 2
    c = lax.rem(me_s, 2)
    lab_peers = [lax.rem(me_l + d, L) for d in range(1, L)]
    seq_peers = [lax.rem(me_s + d, S) for d in range(1, S)]
    side = me_l // half
    inward = me_l + 1 - 2 * side
    outward = lax.rem(me_l - 1 + 2 * side + L, L)
    if L == 2:
        inner, middle = False, True
    else:
        inner = jnp.logical_and(me_l != 0, me_l != L - 1)
        middle = jnp.logical_or(me_l == half - 1, me_l == half)
    across = 1 if L == 2 else jnp.where(middle, 1, 0)
    sent = []
    sent_if = []

    def remote(src, dst, send_sem, recv_sem, device):
        return pltpu.make_async_remote_copy(
            src_ref=src,
            dst_ref=dst,
            send_sem=send_sem,
            recv_sem=recv_sem,
            device_id=device,
            device_id_type=MESH,
        )

    def send(src, dst, sems, index, device):
        copy = remote(src, dst, sems.at[(0,) + index], sems.at[(1,) + index], device)
        copy.start()
        sent.append(copy)
        return copy

    barrier = pltpu.get_barrier_semaphore()
    def greet(peer):
        pl.semaphore_signal(barrier, inc=1, device_id={"lab": peer}, device_id_type=MESH)

    greet(inward)
    when(inner, lambda: greet(outward))
    greetings = S + (0 if L == 2 else jnp.where(inner, 1, 0))

    for peer in seq_peers:
        pl.semaphore_signal(barrier, inc=1, device_id={"seq": peer}, device_id_type=MESH)

    def load(k, src, dst):
        copy = pltpu.make_async_copy(src, dst, load_sem.at[k])
        copy.start()
        return copy

    proj_load = load(0, proj_h, proj)
    hidden_loads = []
    for u in range(NU):
        at = pl.ds(u * unit, unit)
        hidden_loads.append(pltpu.make_async_copy(hidden_h.at[at], hidden.at[at], hidden_sem.at[u]))
        hidden_loads[-1].start()
    counts_load = load(1, counts_h, counts)
    bias_load = load(2, bias_h, bias)
    labels_load = load(3, labels_h, labels)

    def piece(k):
        if isinstance(k, int):
            return pl.ds(k * chunk, chunk)
        return rows(k * chunk, chunk, chunk)

    class Chain:
        def __init__(self, own, arrived, final, up, down, finish):
            self.own, self.arrived, self.final = own, arrived, final
            self.up, self.down, self.finish = up, down, finish

        def up_copy(self, k, slot):
            return remote(
                self.own.at[piece(k)], self.arrived.at[slot, piece(k)],
                self.up.at[2, k], self.up.at[slot, k], {"lab": inward},
            )

        def down_copy(self, k):
            at = self.final.at[piece(k)]
            return remote(at, at, self.down.at[0, k], self.down.at[1, k], {"lab": outward})

        def send_up(self, k):
            self.up_copy(k, across).start()

        def start_unit(self, u):
            def body():
                for i in range(per_unit):
                    self.send_up(u * per_unit + i)

            when(negate(inner), body)

        def sum_with(self, at, slot):
            return self.own[at, :].astype(F32) + self.arrived[slot, at, :].astype(F32)

        def add_up(self, k):
            self.up_copy(k, 0).wait_recv()
            at = piece(k)
            self.own[at, :] = self.sum_with(at, 0).astype(BF16)
            self.send_up(k)

        def settle(self, k, is_middle):
            def meet():
                self.up_copy(k, 1).wait_recv()
                at = piece(k)
                self.final[at, :] = self.finish(self.sum_with(at, 1), at).astype(BF16)

            when(is_middle, meet)
            when(negate(is_middle), lambda: self.down_copy(k).wait_recv())

        def inner_steps(self, first, last, lag, beside={}):
            def body():
                for k in range(first, last):
                    if k < NC:
                        self.add_up(k)
                    if k >= lag:
                        self.settle(k - lag, True if L == 4 else middle)
                        self.down_copy(k - lag).start()
                    if k in beside:
                        beside[k]()

            when(inner, body)

        def outer_wait(self, first, count):
            def body():
                for i in range(count):
                    self.settle(first + i, L == 2)

            when(negate(inner), body)

        def drain(self):
            for k in range(NC):
                self.up_copy(k, 0).wait_send()

            def body():
                for k in range(NC):
                    self.down_copy(k).wait_send()

            when(inner, body)

    def finish_latent(total, at):
        return jnp.tanh(total)

    forward = Chain(own1, in1, lat, up1_sem, down1_sem, finish_latent)

    proj_load.wait()
    for u in range(NU):
        hidden_loads[u].wait()
        at = pl.ds(u * unit, unit)
        own1[at, :] = nn(hidden[at, :], proj[...]).astype(BF16)
        if u == 0:
            pl.semaphore_wait(barrier, greetings)
        forward.start_unit(u)
    queries_load = load(4, queries_h, queries)
    codew_load = load(5, codew_h, codew)
    counts_load.wait()
    cnt[me_s] = counts[...].astype(F32)
    cnt_copies = [
        send(cnt.at[me_s], cnt.at[me_s], cnt_sem, (d,), {"seq": p})
        for d, p in enumerate(seq_peers)
    ]
    tot[me_s] = jnp.zeros((2, C), F32)
    lag = min(LAG_FWD, NC)
    forward.inner_steps(0, NC + lag, lag)
    for copy in cnt_copies:
        copy.wait_recv()
    occurrences = jnp.ones((1, C), F32)
    for s in range(S):
        occurrences = occurrences + cnt[s]
    class_weight = (1.0 - balance_beta) / -expm1(occurrences * math.log(balance_beta))
    cw_row[...] = class_weight
    cw_sum[me_l] = jnp.broadcast_to(jnp.sum(class_weight, 1, keepdims=True), (1, 128))
    queries_load.wait()
    codew_load.wait()

    @pl.loop(0, NU)
    def _(u):
        forward.outer_wait(u * per_unit, per_unit)
        at = rows(u * unit, unit, unit)
        block = lat[at, :]
        weights = jnp.exp(nt(block, queries[...]))
        values = nt(block, codew[...])
        w_s[at, :] = weights
        v_s[at, :] = values
        tot[me_s, 0:1, :] += jnp.sum(weights, 0, keepdims=True)
        tot[me_s, 1:2, :] += jnp.sum(weights * values, 0, keepdims=True)

    note = me_s // per_note
    sister_at = note * per_note

    def tot_copy(target, index):
        return remote(
            tot.at[me_s], tot.at[me_s], tot_sem.at[0, index], tot_sem.at[1, me_s],
            {"seq": target},
        )

    tot_sends = []
    for i in range(1, per_note):
        target = sister_at + lax.rem(me_s - sister_at + i, per_note)
        tot_sends.append(tot_copy(target, len(tot_sends)))
        tot_sends[-1].start()
    others = lax.rem(sister_at + per_note, S)
    for i in range(S - per_note):
        target = lax.rem(others + i, S)
        tot_sends.append(tot_copy(target, len(tot_sends)))
        tot_sends[-1].start()

    def tot_wait(source):
        remote(
            tot.at[source], tot.at[source], tot_sem.at[0, 0], tot_sem.at[1, source],
            {"seq": seq_peers[0]},
        ).wait_recv()

    cw_copies = [
        send(cw_sum.at[me_l], cw_sum.at[me_l], cw_sem, (d,), {"lab": p})
        for d, p in enumerate(lab_peers)
    ]

    bias_load.wait()
    labels_load.wait()
    for i in range(1, per_note):
        tot_wait(sister_at + lax.rem(me_s - sister_at + i, per_note))

    def logits(n):
        both = tot[n * per_note]
        for i in range(1, per_note):
            both = both + tot[n * per_note + i]
        mean = both[1:2, :] / both[0:1, :]
        logit = mean + bias[...][None, :]
        y = labels[pl.ds(n, 1), :].astype(F32)
        t = jnp.exp(-jnp.abs(logit))
        l1p = jnp.log1p(t)
        big = 1.0 / (1.0 + t)
        small = t / (1.0 + t)
        p = jnp.where(logit >= 0, big, small)
        q = jnp.where(logit >= 0, small, big)
        ls_pos = jnp.minimum(logit, 0.0) - l1p
        ls_neg = jnp.minimum(-logit, 0.0) - l1p
        focal = -(y * q * q * ls_pos + (1.0 - y) * p * p * ls_neg)
        slope = -(
            y * q * q * (q - 2.0 * p * ls_pos)
            + (1.0 - y) * p * p * (2.0 * q * ls_neg - p)
        )
        return both[0:1, :], mean, focal, slope

    denominator, mean, _, slope = logits(note)
    gd_row[...] = cw_row[...] * slope / denominator
    mean_row[...] = mean

    def finish_grad(total, at):
        wide = lat[at, :].astype(F32)
        return total * factor * (1.0 - wide * wide)

    sister = {"seq": x * 2 + (1 - c)}
    slots = list(range(1, X)) + [0]
    xs = [lax.rem(x + d, X) for d in range(X)]

    def block(ref, k):
        size = ref.shape[0] // S
        return rows(k * size, size, 16)

    def stage1_copy(a, part, first, d):
        k = xs[d] * 2 + (1 - c)
        return remote(
            part.at[block(part, k)], first.at[d],
            st1_sem.at[0, a, d], st1_sem.at[1, a, d], sister,
        )

    def stage1_slot(a, part, first, d):
        copy = stage1_copy(a, part, first, d)
        copy.start()
        sent.append(copy)
        return copy

    def stage2(a, part, first, mid, second, arrived):
        out = []
        for d in range(1, X):
            arrived[d].wait_recv()
            mine = part[block(part, xs[d] * 2 + c), :].astype(F32)
            mid[d - 1] = (mine + first[d].astype(F32)).astype(BF16)
            out.append(
                send(
                    mid.at[d - 1], second.at[d - 1], st2_sem, (a, d - 1),
                    {"seq": xs[d] * 2 + c},
                )
            )
        return out

    def finish(part, first, second, arrived, copies, scale, out):
        arrived[0].wait_recv()
        total = part[block(part, me_s), :].astype(F32) + first[0].astype(F32)
        for d, copy in enumerate(copies):
            copy.wait_recv()
            total = total + second[d].astype(F32)
        out[...] = (total * scale).astype(BF16)

    backward = Chain(own2, in2, pg, up2_sem, down2_sem, finish_grad)

    @pl.loop(0, NU)
    def _(u):
        at = rows(u * unit, unit, unit)
        value_part = w_s[at, :] * gd_row[...]
        score_part = value_part * (v_s[at, :] - mean_row[...])
        vg = value_part.astype(BF16)
        sg = score_part.astype(BF16)
        vg_s[at, :] = vg
        sg_s[at, :] = sg
        own2[at, :] = (nn(sg, queries[...]) + nn(vg, codew[...])).astype(BF16)
        backward.start_unit(u)

    pw[...] = tn(vg_s[...], lat[...]).astype(BF16)
    w_first = {d: stage1_slot(1, pw, w1, d) for d in range(1, X)}
    q_first = {d: stage1_copy(0, pq, q1, d) for d in slots}
    w_first[0] = stage1_copy(1, pw, w1, 0)
    later = [q_first[d] for d in range(1, X)] + [w_first[0], q_first[0]]
    sent.extend(later)

    def start_later():
        for copy in later:
            copy.start()

    def query_part(i):
        width = C // Q_PARTS
        at = pl.ds(i * width, width)
        pq[at, :] = tn(sg_s[:, at], lat[...]).astype(BF16)

    def query_whole():
        pq[...] = tn(sg_s[...], lat[...]).astype(BF16)
        start_later()

    when(negate(inner), query_whole)
    beside = {Q_AT[i]: functools.partial(query_part, i) for i in range(Q_PARTS)}
    beside[Q_AT[-1]] = start_later

    for copy in cw_copies:
        copy.wait_recv()
    cw_total = cw_sum[0]
    for j in range(1, L):
        cw_total = cw_total + cw_sum[j]
    factor = all_codes / cw_total[0:1, 0:1]
    lag = min(LAG_BWD, NC)
    backward.inner_steps(0, MEET_W, lag, beside)
    w_second = stage2(1, pw, w1, ws, w2, w_first)
    backward.inner_steps(MEET_W, MEET_Q, lag, beside)
    q_second = stage2(0, pq, q1, qs, q2, q_first)
    backward.inner_steps(MEET_Q, NC + lag, lag, beside)

    for i in range(S - per_note):
        tot_wait(lax.rem(others + i, S))
    bias_grad = jnp.zeros((1, C), F32)
    for n in range(notes):
        _, _, focal, slope = logits(n)
        bias_grad = bias_grad + cw_row[...] * slope
        loss_s[me_l, n : n + 1, :] = jnp.broadcast_to(
            jnp.sum(focal * cw_row[...], 1, keepdims=True), (1, 128)
        )
    gb_out[...] = (bias_grad * factor)[0, :]
    loss_copies = [
        send(loss_s.at[me_l], loss_s.at[me_l], loss_sem, (d,), {"lab": p})
        for d, p in enumerate(lab_peers)
    ]
    forward.drain()

    early = (NU - 1) * unit
    wide_block = 2 * (D // S)
    by_slot = wide_block % 128 == 0
    if early:
        backward.outer_wait(0, early // chunk)
        pp32[...] = tn(hidden[0:early, :], pg[0:early, :])
    else:
        pp32[...] = jnp.zeros_like(pp32)
    backward.outer_wait(early // chunk, per_unit)
    p_first = {}
    if by_slot:
        for d in slots:
            at = rows(xs[d] * wide_block, wide_block, 128)
            pp[at, :] = (pp32[at, :] + tn(hidden[early:T, at], pg[early:T, :])).astype(BF16)
            p_first[d] = stage1_slot(2, pp, p1, d)
    else:
        pp[...] = (pp32[...] + tn(hidden[early:T, :], pg[early:T, :])).astype(BF16)
        p_first = {d: stage1_slot(2, pp, p1, d) for d in slots}
    p_second = stage2(2, pp, p1, ps, p2, p_first)
    gh_out[...] = nt(pg[...], proj[...]).astype(BF16)
    finish(pw, w1, w2, w_first, w_second, factor, gw_out)
    finish(pq, q1, q2, q_first, q_second, factor, gq_out)
    for copy in loss_copies:
        copy.wait_recv()
    loss = loss_s[0]
    for j in range(1, L):
        loss = loss + loss_s[j]
    loss_out[...] = loss * factor
    backward.drain()
    for copy in tot_sends:
        copy.wait_send()
    finish(pp, p1, p2, p_first, p_second, 1.0, gp_out)
    for copy in sent:
        copy.wait_send()


def finish_kernel(
    loss, gh, gp, gq, gw, gb, loss_out, gh_out, gp_out, gq_out, gw_out, gb_out, loss_s, sem
):
    pairs = [(gh, gh_out), (gq, gq_out), (gw, gw_out), (gp, gp_out), (gb, gb_out), (loss_s, loss_out)]
    copies = [pltpu.make_async_copy(src, dst, sem.at[k]) for k, (src, dst) in enumerate(pairs)]
    for copy in copies[:-1]:
        copy.start()
    for n in range(loss_s.shape[0]):
        loss_s[n] = jnp.max(loss[n : n + 1, :])
    copies[-1].start()
    for copy in copies:
        copy.wait()


def per_device(hidden, proj_weight, queries, code_weight, code_bias, labels, code_counts):
    L = lax.axis_size("lab")
    S = lax.axis_size("seq")
    X = S // 2
    T, D = hidden.shape
    C, E = queries.shape
    notes = labels.shape[0]
    NU = T // fit(T, UNIT)
    NC = T // fit(fit(T, UNIT), CHUNK)
    vmem = pltpu.VMEM
    dma = pltpu.SemaphoreType.DMA
    scratch = [
        vmem((T, D), BF16),
        vmem((D, E), BF16),
        vmem((C, E), BF16),
        vmem((C, E), BF16),
        vmem((C,), F32),
        vmem((notes, C), jnp.int32),
        vmem((1, C), jnp.int32),
        dma((6,)),
        dma((NU,)),
        vmem((T, E), BF16),
        vmem((2, T, E), BF16),
        vmem((T, E), BF16),
        vmem((T, E), BF16),
        vmem((2, T, E), BF16),
        vmem((T, E), BF16),
        vmem((T, C), F32),
        vmem((T, C), F32),
        vmem((S, 2, C), F32),
        vmem((S, 1, C), F32),
        vmem((L, 1, 128), F32),
        vmem((L, notes, 128), F32),
        vmem((1, C), F32),
        vmem((1, C), F32),
        vmem((1, C), F32),
        vmem((T, C), BF16),
        vmem((T, C), BF16),
        vmem((C, E), BF16),
        vmem((C, E), BF16),
        vmem((D, E), BF16),
        vmem((D, E), F32),
        vmem((X, C // S, E), BF16),
        vmem((X, C // S, E), BF16),
        vmem((X, D // S, E), BF16),
        vmem((X - 1, C // S, E), BF16),
        vmem((X - 1, C // S, E), BF16),
        vmem((X - 1, D // S, E), BF16),
        vmem((X - 1, C // S, E), BF16),
        vmem((X - 1, C // S, E), BF16),
        vmem((X - 1, D // S, E), BF16),
        dma((2, S - 1)),
        dma((2, S)),
        dma((2, L - 1)),
        dma((2, L - 1)),
        dma((3, NC)),
        dma((2, NC)),
        dma((3, NC)),
        dma((2, NC)),
        dma((2, 3, X)),
        dma((2, 3, X - 1)),
    ]
    whole = pl.BlockSpec(memory_space=pltpu.VMEM)
    anywhere = pl.BlockSpec(memory_space=pl.ANY)
    outs = pl.pallas_call(
        functools.partial(kernel, S, L, float(C * L)),
        out_shape=(
            pltpu.VMEM((notes, 128), F32),
            pltpu.VMEM((T, D), BF16),
            pltpu.VMEM((D // S, E), BF16),
            pltpu.VMEM((C // S, E), BF16),
            pltpu.VMEM((C // S, E), BF16),
            pltpu.VMEM((C,), F32),
        ),
        in_specs=[anywhere] * 7,
        scratch_shapes=scratch,
        compiler_params=pltpu.CompilerParams(
            collective_id=0, has_side_effects=True, vmem_limit_bytes=54 * 1024 * 1024
        ),
    )(hidden, proj_weight, queries, code_weight, code_bias, labels, code_counts)
    return pl.pallas_call(
        finish_kernel,
        out_shape=(
            jax.ShapeDtypeStruct((notes,), F32),
            jax.ShapeDtypeStruct((T, D), BF16),
            jax.ShapeDtypeStruct((D // S, E), BF16),
            jax.ShapeDtypeStruct((C // S, E), BF16),
            jax.ShapeDtypeStruct((C // S, E), BF16),
            jax.ShapeDtypeStruct((C,), F32),
        ),
        in_specs=[whole] * 6,
        out_specs=(anywhere,) * 6,
        scratch_shapes=[pltpu.SMEM((notes,), F32), dma((6,))],
    )(*(pltpu.with_memory_space_constraint(out, pltpu.VMEM) for out in outs))


def solution(mesh):
    placed = (
        P(("grp", "seq"), "lab"),
        P("lab", None),
        P("lab", None),
        P("lab", None),
        P("lab"),
        P("grp", "lab"),
        P(("grp", "seq"), "lab"),
    )
    return jax.shard_map(
        per_device,
        mesh=mesh,
        in_specs=placed,
        out_specs=(
            P("grp"),
            P(("grp", "seq"), "lab"),
            P(("grp", "lab", "seq"), None),
            P(("grp", "lab", "seq"), None),
            P(("grp", "lab", "seq"), None),
            P(("grp", "lab")),
        ),
        check_vma=False,
    )
```

```python
import functools
import math

import jax
import jax.numpy as jnp
from jax import lax
from jax.experimental import pallas as pl
from jax.experimental.pallas import tpu as pltpu
from jax.sharding import PartitionSpec as P

balance_beta = 0.9999
MESH = pl.DeviceIdType.MESH
F32 = jnp.float32
BF16 = jnp.bfloat16
CHUNK = 64
UNIT = 256
LAG_FWD = 5
LAG_BWD = 5
MEET_W = 3
MEET_Q = 12
Q_PARTS = 3
Q_AT = (1, 4, 6, 7)


def expm1(x):
    series = jnp.ones_like(x)
    for order in range(10, 1, -1):
        series = 1.0 + x * series * (1.0 / order)
    return jnp.where(jnp.abs(x) < 0.5, x * series, jnp.exp(x) - 1.0)


def nt(a, b):
    return lax.dot_general(a, b, (((1,), (1,)), ((), ())), preferred_element_type=F32)


def tn(a, b):
    return lax.dot_general(a, b, (((0,), (0,)), ((), ())), preferred_element_type=F32)


def nn(a, b):
    return jnp.dot(a, b, preferred_element_type=F32)


def rows(start, size, multiple):
    return pl.ds(pl.multiple_of(start, multiple), size)


def fit(size, want):
    return want if size % want == 0 else size


def both_true(a, b):
    if isinstance(a, bool):
        return b if a else False
    if isinstance(b, bool):
        return a if b else False
    return jnp.logical_and(a, b)


def negate(a):
    return (not a) if isinstance(a, bool) else jnp.logical_not(a)


def when(condition, body):
    if isinstance(condition, bool):
        if condition:
            body()
    else:
        pl.when(condition)(body)


def far_first(count):
    return sorted(range(1, count), key=lambda d: -min(d, count - d))


def kernel(
    S, L, all_codes,
    hidden_h, proj_h, queries_h, codew_h, bias_h, labels_h, counts_h,
    loss_out, gh_out, gp_out, gq_out, gw_out, gb_out,
    hidden, proj, queries, codew, bias, labels, counts, load_sem, hidden_sem, own1, in1, lat, own2, in2, pg,
    w_s, v_s, tot, cnt, cw_sum, loss_s, cw_row, inverse_row, grad_row, mean_row, sg_s, vg_s,
    pq, pw, pp, pp32, q1, w1, p1, qs, ws, ps, q2, w2, p2,
    cnt_sem, tot_sem, cw_sem, loss_sem, up1_sem, down1_sem, up2_sem, down2_sem, st1_sem, st2_sem,
):
    T, D = hidden.shape
    C, E = queries.shape
    notes = labels.shape[0]
    X = S // 2
    per_note = S // notes
    unit = fit(T, UNIT)
    chunk = fit(unit, CHUNK)
    NC = T // chunk
    NU = T // unit
    per_unit = unit // chunk
    half = L // 2
    me_s = lax.axis_index("seq")
    me_l = lax.axis_index("lab")
    x = me_s // 2
    c = lax.rem(me_s, 2)
    lab_peers = [lax.rem(me_l + d, L) for d in range(1, L)]
    seq_peers = [lax.rem(me_s + d, S) for d in range(1, S)]
    side = me_l // half
    inward = me_l + 1 - 2 * side
    outward = lax.rem(me_l - 1 + 2 * side + L, L)
    if L == 2:
        inner, middle = False, True
    else:
        inner = jnp.logical_and(me_l != 0, me_l != L - 1)
        middle = jnp.logical_or(me_l == half - 1, me_l == half)
    across = 1 if L == 2 else jnp.where(middle, 1, 0)
    sent = []
    sent_if = []

    def remote(src, dst, send_sem, recv_sem, device):
        return pltpu.make_async_remote_copy(
            src_ref=src,
            dst_ref=dst,
            send_sem=send_sem,
            recv_sem=recv_sem,
            device_id=device,
            device_id_type=MESH,
        )

    def send(src, dst, sems, index, device):
        copy = remote(src, dst, sems.at[(0,) + index], sems.at[(1,) + index], device)
        copy.start()
        sent.append(copy)
        return copy

    barrier = pltpu.get_barrier_semaphore()
    def greet(peer):
        pl.semaphore_signal(barrier, inc=1, device_id={"lab": peer}, device_id_type=MESH)

    greet(inward)
    when(inner, lambda: greet(outward))
    greetings = S + (0 if L == 2 else jnp.where(inner, 1, 0))

    for peer in seq_peers:
        pl.semaphore_signal(barrier, inc=1, device_id={"seq": peer}, device_id_type=MESH)

    def load(k, src, dst):
        copy = pltpu.make_async_copy(src, dst, load_sem.at[k])
        copy.start()
        return copy

    proj_load = load(0, proj_h, proj)
    hidden_loads = []
    for u in range(NU):
        at = pl.ds(u * unit, unit)
        hidden_loads.append(pltpu.make_async_copy(hidden_h.at[at], hidden.at[at], hidden_sem.at[u]))
        hidden_loads[-1].start()
    counts_load = load(1, counts_h, counts)
    bias_load = load(2, bias_h, bias)
    labels_load = load(3, labels_h, labels)

    def piece(k):
        if isinstance(k, int):
            return pl.ds(k * chunk, chunk)
        return rows(k * chunk, chunk, chunk)

    class Chain:
        def __init__(self, own, arrived, final, up, down, finish):
            self.own, self.arrived, self.final = own, arrived, final
            self.up, self.down, self.finish = up, down, finish

        def up_copy(self, k, slot):
            return remote(
                self.own.at[piece(k)], self.arrived.at[slot, piece(k)],
                self.up.at[2, k], self.up.at[slot, k], {"lab": inward},
            )

        def down_copy(self, k):
            at = self.final.at[piece(k)]
            return remote(at, at, self.down.at[0, k], self.down.at[1, k], {"lab": outward})

        def send_up(self, k):
            self.up_copy(k, across).start()

        def start_unit(self, u):
            def body():
                for i in range(per_unit):
                    self.send_up(u * per_unit + i)

            when(negate(inner), body)

        def sum_with(self, at, slot):
            return self.own[at, :].astype(F32) + self.arrived[slot, at, :].astype(F32)

        def add_up(self, k):
            self.up_copy(k, 0).wait_recv()
            at = piece(k)
            self.own[at, :] = self.sum_with(at, 0).astype(BF16)
            self.send_up(k)

        def settle(self, k, is_middle):
            def meet():
                self.up_copy(k, 1).wait_recv()
                at = piece(k)
                self.final[at, :] = self.finish(self.sum_with(at, 1), at).astype(BF16)

            when(is_middle, meet)
            when(negate(is_middle), lambda: self.down_copy(k).wait_recv())

        def inner_steps(self, first, last, lag, beside={}):
            def body():
                for k in range(first, last):
                    if k < NC:
                        self.add_up(k)
                    if k >= lag:
                        self.settle(k - lag, True if L == 4 else middle)
                        self.down_copy(k - lag).start()
                    if k in beside:
                        beside[k]()

            when(inner, body)

        def outer_wait(self, first, count):
            def body():
                for i in range(count):
                    self.settle(first + i, L == 2)

            when(negate(inner), body)

        def drain(self):
            for k in range(NC):
                self.up_copy(k, 0).wait_send()

            def body():
                for k in range(NC):
                    self.down_copy(k).wait_send()

            when(inner, body)

    def finish_latent(total, at):
        return jnp.tanh(total)

    forward = Chain(own1, in1, lat, up1_sem, down1_sem, finish_latent)

    proj_load.wait()
    for u in range(NU):
        hidden_loads[u].wait()
        at = pl.ds(u * unit, unit)
        own1[at, :] = nn(hidden[at, :], proj[...]).astype(BF16)
        if u == 0:
            pl.semaphore_wait(barrier, greetings)
        forward.start_unit(u)
    queries_load = load(4, queries_h, queries)
    codew_load = load(5, codew_h, codew)
    counts_load.wait()
    cnt[me_s] = counts[...].astype(F32)
    cnt_copies = [
        send(cnt.at[me_s], cnt.at[me_s], cnt_sem, (d,), {"seq": p})
        for d, p in enumerate(seq_peers)
    ]
    tot[me_s] = jnp.zeros((2, C), F32)
    lag = min(LAG_FWD, NC)
    forward.inner_steps(0, NC + lag, lag)
    for copy in cnt_copies:
        copy.wait_recv()
    occurrences = jnp.ones((1, C), F32)
    for s in range(S):
        occurrences = occurrences + cnt[s]
    class_weight = (1.0 - balance_beta) / -expm1(occurrences * math.log(balance_beta))
    cw_row[...] = class_weight
    cw_sum[me_l] = jnp.broadcast_to(jnp.sum(class_weight, 1, keepdims=True), (1, 128))
    queries_load.wait()
    codew_load.wait()

    @pl.loop(0, NU)
    def _(u):
        forward.outer_wait(u * per_unit, per_unit)
        at = rows(u * unit, unit, unit)
        block = lat[at, :]
        weights = jnp.exp(nt(block, queries[...]))
        values = nt(block, codew[...])
        w_s[at, :] = weights
        v_s[at, :] = values
        tot[me_s, 0:1, :] += jnp.sum(weights, 0, keepdims=True)
        tot[me_s, 1:2, :] += jnp.sum(weights * values, 0, keepdims=True)

    note = me_s // per_note
    sister_at = note * per_note

    def tot_copy(target, index):
        return remote(
            tot.at[me_s], tot.at[me_s], tot_sem.at[0, index], tot_sem.at[1, me_s],
            {"seq": target},
        )

    tot_sends = []
    for i in range(1, per_note):
        target = sister_at + lax.rem(me_s - sister_at + i, per_note)
        tot_sends.append(tot_copy(target, len(tot_sends)))
        tot_sends[-1].start()
    others = lax.rem(sister_at + per_note, S)
    for i in range(S - per_note):
        target = lax.rem(others + i, S)
        tot_sends.append(tot_copy(target, len(tot_sends)))
        tot_sends[-1].start()

    def tot_wait(source):
        remote(
            tot.at[source], tot.at[source], tot_sem.at[0, 0], tot_sem.at[1, source],
            {"seq": seq_peers[0]},
        ).wait_recv()

    cw_copies = [
        send(cw_sum.at[me_l], cw_sum.at[me_l], cw_sem, (d,), {"lab": p})
        for d, p in enumerate(lab_peers)
    ]

    bias_load.wait()
    labels_load.wait()
    for i in range(1, per_note):
        tot_wait(sister_at + lax.rem(me_s - sister_at + i, per_note))

    def logits(n):
        both = tot[n * per_note]
        for i in range(1, per_note):
            both = both + tot[n * per_note + i]
        mean = both[1:2, :] / both[0:1, :]
        logit = mean + bias[...][None, :]
        y = labels[pl.ds(n, 1), :].astype(F32)
        t = jnp.exp(-jnp.abs(logit))
        l1p = jnp.log1p(t)
        big = 1.0 / (1.0 + t)
        small = t / (1.0 + t)
        p = jnp.where(logit >= 0, big, small)
        q = jnp.where(logit >= 0, small, big)
        ls_pos = jnp.minimum(logit, 0.0) - l1p
        ls_neg = jnp.minimum(-logit, 0.0) - l1p
        focal = -(y * q * q * ls_pos + (1.0 - y) * p * p * ls_neg)
        slope = -(
            y * q * q * (q - 2.0 * p * ls_pos)
            + (1.0 - y) * p * p * (2.0 * q * ls_neg - p)
        )
        return both[0:1, :], mean, focal, slope

    denominator, mean, _, slope = logits(note)
    inverse_row[...] = 1.0 / denominator
    grad_row[...] = cw_row[...] * slope
    mean_row[...] = mean

    def finish_grad(total, at):
        wide = lat[at, :].astype(F32)
        return total * factor * (1.0 - wide * wide)

    sister = {"seq": x * 2 + (1 - c)}
    slots = list(range(1, X)) + [0]
    xs = [lax.rem(x + d, X) for d in range(X)]

    def block(ref, k):
        size = ref.shape[0] // S
        return rows(k * size, size, 16)

    def stage1_copy(a, part, first, d):
        k = xs[d] * 2 + (1 - c)
        return remote(
            part.at[block(part, k)], first.at[d],
            st1_sem.at[0, a, d], st1_sem.at[1, a, d], sister,
        )

    def stage1_slot(a, part, first, d):
        copy = stage1_copy(a, part, first, d)
        copy.start()
        sent.append(copy)
        return copy

    def stage2(a, part, first, mid, second, arrived):
        out = []
        for d in range(1, X):
            arrived[d].wait_recv()
            mine = part[block(part, xs[d] * 2 + c), :].astype(F32)
            mid[d - 1] = (mine + first[d].astype(F32)).astype(BF16)
            out.append(
                send(
                    mid.at[d - 1], second.at[d - 1], st2_sem, (a, d - 1),
                    {"seq": xs[d] * 2 + c},
                )
            )
        return out

    def finish(part, first, second, arrived, copies, scale, out):
        arrived[0].wait_recv()
        total = part[block(part, me_s), :].astype(F32) + first[0].astype(F32)
        for d, copy in enumerate(copies):
            copy.wait_recv()
            total = total + second[d].astype(F32)
        out[...] = (total * scale).astype(BF16)

    backward = Chain(own2, in2, pg, up2_sem, down2_sem, finish_grad)

    @pl.loop(0, NU)
    def _(u):
        at = rows(u * unit, unit, unit)
        value_part = w_s[at, :] * inverse_row[...] * grad_row[...]
        score_part = value_part * (v_s[at, :] - mean_row[...])
        vg = value_part.astype(BF16)
        sg = score_part.astype(BF16)
        vg_s[at, :] = vg
        sg_s[at, :] = sg
        own2[at, :] = (nn(sg, queries[...]) + nn(vg, codew[...])).astype(BF16)
        backward.start_unit(u)

    pw[...] = tn(vg_s[...], lat[...]).astype(BF16)
    w_first = {d: stage1_slot(1, pw, w1, d) for d in range(1, X)}
    q_first = {d: stage1_copy(0, pq, q1, d) for d in slots}
    w_first[0] = stage1_copy(1, pw, w1, 0)
    later = [q_first[d] for d in range(1, X)] + [w_first[0], q_first[0]]
    sent.extend(later)

    def start_later():
        for copy in later:
            copy.start()

    def query_part(i):
        width = C // Q_PARTS
        at = pl.ds(i * width, width)
        pq[at, :] = tn(sg_s[:, at], lat[...]).astype(BF16)

    def query_whole():
        pq[...] = tn(sg_s[...], lat[...]).astype(BF16)
        start_later()

    when(negate(inner), query_whole)
    beside = {Q_AT[i]: functools.partial(query_part, i) for i in range(Q_PARTS)}
    beside[Q_AT[-1]] = start_later

    for copy in cw_copies:
        copy.wait_recv()
    cw_total = cw_sum[0]
    for j in range(1, L):
        cw_total = cw_total + cw_sum[j]
    factor = all_codes / cw_total[0:1, 0:1]
    lag = min(LAG_BWD, NC)
    backward.inner_steps(0, MEET_W, lag, beside)
    w_second = stage2(1, pw, w1, ws, w2, w_first)
    backward.inner_steps(MEET_W, MEET_Q, lag, beside)
    q_second = stage2(0, pq, q1, qs, q2, q_first)
    backward.inner_steps(MEET_Q, NC + lag, lag, beside)

    for i in range(S - per_note):
        tot_wait(lax.rem(others + i, S))
    bias_grad = jnp.zeros((1, C), F32)
    for n in range(notes):
        _, _, focal, slope = logits(n)
        bias_grad = bias_grad + cw_row[...] * slope
        loss_s[me_l, n : n + 1, :] = jnp.broadcast_to(
            jnp.sum(focal * cw_row[...], 1, keepdims=True), (1, 128)
        )
    gb_out[...] = (bias_grad * factor)[0, :]
    loss_copies = [
        send(loss_s.at[me_l], loss_s.at[me_l], loss_sem, (d,), {"lab": p})
        for d, p in enumerate(lab_peers)
    ]
    forward.drain()

    early = (NU - 1) * unit
    wide_block = 2 * (D // S)
    by_slot = wide_block % 128 == 0
    if early:
        backward.outer_wait(0, early // chunk)
        pp32[...] = tn(hidden[0:early, :], pg[0:early, :])
    else:
        pp32[...] = jnp.zeros_like(pp32)
    backward.outer_wait(early // chunk, per_unit)
    p_first = {}
    if by_slot:
        for d in slots:
            at = rows(xs[d] * wide_block, wide_block, 128)
            pp[at, :] = (pp32[at, :] + tn(hidden[early:T, at], pg[early:T, :])).astype(BF16)
            p_first[d] = stage1_slot(2, pp, p1, d)
    else:
        pp[...] = (pp32[...] + tn(hidden[early:T, :], pg[early:T, :])).astype(BF16)
        p_first = {d: stage1_slot(2, pp, p1, d) for d in slots}
    p_second = stage2(2, pp, p1, ps, p2, p_first)
    gh_out[...] = nt(pg[...], proj[...]).astype(BF16)
    finish(pw, w1, w2, w_first, w_second, factor, gw_out)
    finish(pq, q1, q2, q_first, q_second, factor, gq_out)
    for copy in loss_copies:
        copy.wait_recv()
    loss = loss_s[0]
    for j in range(1, L):
        loss = loss + loss_s[j]
    loss_out[...] = loss * factor
    backward.drain()
    for copy in tot_sends:
        copy.wait_send()
    finish(pp, p1, p2, p_first, p_second, 1.0, gp_out)
    for copy in sent:
        copy.wait_send()


def finish_kernel(
    loss, gh, gp, gq, gw, gb, loss_out, gh_out, gp_out, gq_out, gw_out, gb_out, loss_s, sem
):
    pairs = [(gh, gh_out), (gq, gq_out), (gw, gw_out), (gp, gp_out), (gb, gb_out), (loss_s, loss_out)]
    copies = [pltpu.make_async_copy(src, dst, sem.at[k]) for k, (src, dst) in enumerate(pairs)]
    for copy in copies[:-1]:
        copy.start()
    for n in range(loss_s.shape[0]):
        loss_s[n] = jnp.max(loss[n : n + 1, :])
    copies[-1].start()
    for copy in copies:
        copy.wait()


def per_device(hidden, proj_weight, queries, code_weight, code_bias, labels, code_counts):
    L = lax.axis_size("lab")
    S = lax.axis_size("seq")
    X = S // 2
    T, D = hidden.shape
    C, E = queries.shape
    notes = labels.shape[0]
    NU = T // fit(T, UNIT)
    NC = T // fit(fit(T, UNIT), CHUNK)
    vmem = pltpu.VMEM
    dma = pltpu.SemaphoreType.DMA
    scratch = [
        vmem((T, D), BF16),
        vmem((D, E), BF16),
        vmem((C, E), BF16),
        vmem((C, E), BF16),
        vmem((C,), F32),
        vmem((notes, C), jnp.int32),
        vmem((1, C), jnp.int32),
        dma((6,)),
        dma((NU,)),
        vmem((T, E), BF16),
        vmem((2, T, E), BF16),
        vmem((T, E), BF16),
        vmem((T, E), BF16),
        vmem((2, T, E), BF16),
        vmem((T, E), BF16),
        vmem((T, C), F32),
        vmem((T, C), F32),
        vmem((S, 2, C), F32),
        vmem((S, 1, C), F32),
        vmem((L, 1, 128), F32),
        vmem((L, notes, 128), F32),
        vmem((1, C), F32),
        vmem((1, C), F32),
        vmem((1, C), F32),
        vmem((1, C), F32),
        vmem((T, C), BF16),
        vmem((T, C), BF16),
        vmem((C, E), BF16),
        vmem((C, E), BF16),
        vmem((D, E), BF16),
        vmem((D, E), F32),
        vmem((X, C // S, E), BF16),
        vmem((X, C // S, E), BF16),
        vmem((X, D // S, E), BF16),
        vmem((X - 1, C // S, E), BF16),
        vmem((X - 1, C // S, E), BF16),
        vmem((X - 1, D // S, E), BF16),
        vmem((X - 1, C // S, E), BF16),
        vmem((X - 1, C // S, E), BF16),
        vmem((X - 1, D // S, E), BF16),
        dma((2, S - 1)),
        dma((2, S)),
        dma((2, L - 1)),
        dma((2, L - 1)),
        dma((3, NC)),
        dma((2, NC)),
        dma((3, NC)),
        dma((2, NC)),
        dma((2, 3, X)),
        dma((2, 3, X - 1)),
    ]
    whole = pl.BlockSpec(memory_space=pltpu.VMEM)
    anywhere = pl.BlockSpec(memory_space=pl.ANY)
    outs = pl.pallas_call(
        functools.partial(kernel, S, L, float(C * L)),
        out_shape=(
            pltpu.VMEM((notes, 128), F32),
            pltpu.VMEM((T, D), BF16),
            pltpu.VMEM((D // S, E), BF16),
            pltpu.VMEM((C // S, E), BF16),
            pltpu.VMEM((C // S, E), BF16),
            pltpu.VMEM((C,), F32),
        ),
        in_specs=[anywhere] * 7,
        scratch_shapes=scratch,
        compiler_params=pltpu.CompilerParams(
            collective_id=0, has_side_effects=True, vmem_limit_bytes=54 * 1024 * 1024
        ),
    )(hidden, proj_weight, queries, code_weight, code_bias, labels, code_counts)
    return pl.pallas_call(
        finish_kernel,
        out_shape=(
            jax.ShapeDtypeStruct((notes,), F32),
            jax.ShapeDtypeStruct((T, D), BF16),
            jax.ShapeDtypeStruct((D // S, E), BF16),
            jax.ShapeDtypeStruct((C // S, E), BF16),
            jax.ShapeDtypeStruct((C // S, E), BF16),
            jax.ShapeDtypeStruct((C,), F32),
        ),
        in_specs=[whole] * 6,
        out_specs=(anywhere,) * 6,
        scratch_shapes=[pltpu.SMEM((notes,), F32), dma((6,))],
    )(*(pltpu.with_memory_space_constraint(out, pltpu.VMEM) for out in outs))


def solution(mesh):
    placed = (
        P(("grp", "seq"), "lab"),
        P("lab", None),
        P("lab", None),
        P("lab", None),
        P("lab"),
        P("grp", "lab"),
        P(("grp", "seq"), "lab"),
    )
    return jax.shard_map(
        per_device,
        mesh=mesh,
        in_specs=placed,
        out_specs=(
            P("grp"),
            P(("grp", "seq"), "lab"),
            P(("grp", "lab", "seq"), None),
            P(("grp", "lab", "seq"), None),
            P(("grp", "lab", "seq"), None),
            P(("grp", "lab")),
        ),
        check_vma=False,
    )
```

```python
import functools
import math

import jax
import jax.numpy as jnp
from jax import lax
from jax.experimental import pallas as pl
from jax.experimental.pallas import tpu as pltpu
from jax.sharding import PartitionSpec as P

balance_beta = 0.9999
MESH = pl.DeviceIdType.MESH
F32 = jnp.float32
BF16 = jnp.bfloat16
CHUNK = 64
UNIT = 256
LAG_FWD = 4
LAG_BWD = 5
MEET_W = 3
MEET_Q = 12
Q_PARTS = 3
Q_AT = (1, 4, 6, 7)


def expm1(x):
    series = jnp.ones_like(x)
    for order in range(10, 1, -1):
        series = 1.0 + x * series * (1.0 / order)
    return jnp.where(jnp.abs(x) < 0.5, x * series, jnp.exp(x) - 1.0)


def nt(a, b):
    return lax.dot_general(a, b, (((1,), (1,)), ((), ())), preferred_element_type=F32)


def tn(a, b):
    return lax.dot_general(a, b, (((0,), (0,)), ((), ())), preferred_element_type=F32)


def nn(a, b):
    return jnp.dot(a, b, preferred_element_type=F32)


def rows(start, size, multiple):
    return pl.ds(pl.multiple_of(start, multiple), size)


def fit(size, want):
    return want if size % want == 0 else size


def both_true(a, b):
    if isinstance(a, bool):
        return b if a else False
    if isinstance(b, bool):
        return a if b else False
    return jnp.logical_and(a, b)


def negate(a):
    return (not a) if isinstance(a, bool) else jnp.logical_not(a)


def when(condition, body):
    if isinstance(condition, bool):
        if condition:
            body()
    else:
        pl.when(condition)(body)


def far_first(count):
    return sorted(range(1, count), key=lambda d: -min(d, count - d))


def kernel(
    S, L, all_codes,
    hidden_h, proj_h, queries_h, codew_h, bias_h, labels_h, counts_h,
    loss_out, gh_out, gp_out, gq_out, gw_out, gb_out,
    hidden, proj, queries, codew, bias, labels, counts, load_sem, hidden_sem, own1, in1, lat, own2, in2, pg,
    w_s, v_s, tot, cnt, cw_sum, loss_s, cw_row, inverse_row, grad_row, mean_row, sg_s, vg_s,
    pq, pw, pp, pp32, q1, w1, p1, qs, ws, ps, q2, w2, p2,
    cnt_sem, tot_sem, cw_sem, loss_sem, up1_sem, down1_sem, up2_sem, down2_sem, st1_sem, st2_sem,
):
    T, D = hidden.shape
    C, E = queries.shape
    notes = labels.shape[0]
    X = S // 2
    per_note = S // notes
    unit = fit(T, UNIT)
    chunk = fit(unit, CHUNK)
    NC = T // chunk
    NU = T // unit
    per_unit = unit // chunk
    half = L // 2
    me_s = lax.axis_index("seq")
    me_l = lax.axis_index("lab")
    x = me_s // 2
    c = lax.rem(me_s, 2)
    lab_peers = [lax.rem(me_l + d, L) for d in range(1, L)]
    seq_peers = [lax.rem(me_s + d, S) for d in range(1, S)]
    side = me_l // half
    inward = me_l + 1 - 2 * side
    outward = lax.rem(me_l - 1 + 2 * side + L, L)
    if L == 2:
        inner, middle = False, True
    else:
        inner = jnp.logical_and(me_l != 0, me_l != L - 1)
        middle = jnp.logical_or(me_l == half - 1, me_l == half)
    across = 1 if L == 2 else jnp.where(middle, 1, 0)
    sent = []
    sent_if = []

    def remote(src, dst, send_sem, recv_sem, device):
        return pltpu.make_async_remote_copy(
            src_ref=src,
            dst_ref=dst,
            send_sem=send_sem,
            recv_sem=recv_sem,
            device_id=device,
            device_id_type=MESH,
        )

    def send(src, dst, sems, index, device):
        copy = remote(src, dst, sems.at[(0,) + index], sems.at[(1,) + index], device)
        copy.start()
        sent.append(copy)
        return copy

    barrier = pltpu.get_barrier_semaphore()
    def greet(peer):
        pl.semaphore_signal(barrier, inc=1, device_id={"lab": peer}, device_id_type=MESH)

    greet(inward)
    when(inner, lambda: greet(outward))
    greetings = S + (0 if L == 2 else jnp.where(inner, 1, 0))

    for peer in seq_peers:
        pl.semaphore_signal(barrier, inc=1, device_id={"seq": peer}, device_id_type=MESH)

    def load(k, src, dst):
        copy = pltpu.make_async_copy(src, dst, load_sem.at[k])
        copy.start()
        return copy

    proj_load = load(0, proj_h, proj)
    hidden_loads = []
    for u in range(NU):
        at = pl.ds(u * unit, unit)
        hidden_loads.append(pltpu.make_async_copy(hidden_h.at[at], hidden.at[at], hidden_sem.at[u]))
        hidden_loads[-1].start()
    counts_load = load(1, counts_h, counts)
    bias_load = load(2, bias_h, bias)
    labels_load = load(3, labels_h, labels)

    def piece(k):
        if isinstance(k, int):
            return pl.ds(k * chunk, chunk)
        return rows(k * chunk, chunk, chunk)

    class Chain:
        def __init__(self, own, arrived, final, up, down, finish):
            self.own, self.arrived, self.final = own, arrived, final
            self.up, self.down, self.finish = up, down, finish

        def up_copy(self, k, slot):
            return remote(
                self.own.at[piece(k)], self.arrived.at[slot, piece(k)],
                self.up.at[2, k], self.up.at[slot, k], {"lab": inward},
            )

        def down_copy(self, k):
            at = self.final.at[piece(k)]
            return remote(at, at, self.down.at[0, k], self.down.at[1, k], {"lab": outward})

        def send_up(self, k):
            self.up_copy(k, across).start()

        def start_unit(self, u):
            def body():
                for i in range(per_unit):
                    self.send_up(u * per_unit + i)

            when(negate(inner), body)

        def sum_with(self, at, slot):
            return self.own[at, :].astype(F32) + self.arrived[slot, at, :].astype(F32)

        def add_up(self, k):
            self.up_copy(k, 0).wait_recv()
            at = piece(k)
            self.own[at, :] = self.sum_with(at, 0).astype(BF16)
            self.send_up(k)

        def settle(self, k, is_middle):
            def meet():
                self.up_copy(k, 1).wait_recv()
                at = piece(k)
                self.final[at, :] = self.finish(self.sum_with(at, 1), at).astype(BF16)

            when(is_middle, meet)
            when(negate(is_middle), lambda: self.down_copy(k).wait_recv())

        def inner_steps(self, first, last, lag, beside={}):
            def body():
                for k in range(first, last):
                    if k < NC:
                        self.add_up(k)
                    if k >= lag:
                        self.settle(k - lag, True if L == 4 else middle)
                        self.down_copy(k - lag).start()
                    if k in beside:
                        beside[k]()

            when(inner, body)

        def outer_wait(self, first, count):
            def body():
                for i in range(count):
                    self.settle(first + i, L == 2)

            when(negate(inner), body)

        def drain(self):
            for k in range(NC):
                self.up_copy(k, 0).wait_send()

            def body():
                for k in range(NC):
                    self.down_copy(k).wait_send()

            when(inner, body)

    def finish_latent(total, at):
        return jnp.tanh(total)

    forward = Chain(own1, in1, lat, up1_sem, down1_sem, finish_latent)

    proj_load.wait()
    for u in range(NU):
        hidden_loads[u].wait()
        at = pl.ds(u * unit, unit)
        own1[at, :] = nn(hidden[at, :], proj[...]).astype(BF16)
        if u == 0:
            pl.semaphore_wait(barrier, greetings)
        forward.start_unit(u)
    queries_load = load(4, queries_h, queries)
    codew_load = load(5, codew_h, codew)
    counts_load.wait()
    cnt[me_s] = counts[...].astype(F32)
    cnt_copies = [
        send(cnt.at[me_s], cnt.at[me_s], cnt_sem, (d,), {"seq": p})
        for d, p in enumerate(seq_peers)
    ]
    tot[me_s] = jnp.zeros((2, C), F32)
    lag = min(LAG_FWD, NC)
    forward.inner_steps(0, NC + lag, lag)
    for copy in cnt_copies:
        copy.wait_recv()
    occurrences = jnp.ones((1, C), F32)
    for s in range(S):
        occurrences = occurrences + cnt[s]
    class_weight = (1.0 - balance_beta) / -expm1(occurrences * math.log(balance_beta))
    cw_row[...] = class_weight
    cw_sum[me_l] = jnp.broadcast_to(jnp.sum(class_weight, 1, keepdims=True), (1, 128))
    queries_load.wait()
    codew_load.wait()

    @pl.loop(0, NU)
    def _(u):
        forward.outer_wait(u * per_unit, per_unit)
        at = rows(u * unit, unit, unit)
        block = lat[at, :]
        weights = jnp.exp(nt(block, queries[...]))
        values = nt(block, codew[...])
        w_s[at, :] = weights
        v_s[at, :] = values
        tot[me_s, 0:1, :] += jnp.sum(weights, 0, keepdims=True)
        tot[me_s, 1:2, :] += jnp.sum(weights * values, 0, keepdims=True)

    note = me_s // per_note
    sister_at = note * per_note

    def tot_copy(target, index):
        return remote(
            tot.at[me_s], tot.at[me_s], tot_sem.at[0, index], tot_sem.at[1, me_s],
            {"seq": target},
        )

    tot_sends = []
    for i in range(1, per_note):
        target = sister_at + lax.rem(me_s - sister_at + i, per_note)
        tot_sends.append(tot_copy(target, len(tot_sends)))
        tot_sends[-1].start()
    others = lax.rem(sister_at + per_note, S)
    for i in range(S - per_note):
        target = lax.rem(others + i, S)
        tot_sends.append(tot_copy(target, len(tot_sends)))
        tot_sends[-1].start()

    def tot_wait(source):
        remote(
            tot.at[source], tot.at[source], tot_sem.at[0, 0], tot_sem.at[1, source],
            {"seq": seq_peers[0]},
        ).wait_recv()

    cw_copies = [
        send(cw_sum.at[me_l], cw_sum.at[me_l], cw_sem, (d,), {"lab": p})
        for d, p in enumerate(lab_peers)
    ]

    bias_load.wait()
    labels_load.wait()
    for i in range(1, per_note):
        tot_wait(sister_at + lax.rem(me_s - sister_at + i, per_note))

    def logits(n):
        both = tot[n * per_note]
        for i in range(1, per_note):
            both = both + tot[n * per_note + i]
        mean = both[1:2, :] / both[0:1, :]
        logit = mean + bias[...][None, :]
        y = labels[pl.ds(n, 1), :].astype(F32)
        t = jnp.exp(-jnp.abs(logit))
        l1p = jnp.log1p(t)
        big = 1.0 / (1.0 + t)
        small = t / (1.0 + t)
        p = jnp.where(logit >= 0, big, small)
        q = jnp.where(logit >= 0, small, big)
        ls_pos = jnp.minimum(logit, 0.0) - l1p
        ls_neg = jnp.minimum(-logit, 0.0) - l1p
        focal = -(y * q * q * ls_pos + (1.0 - y) * p * p * ls_neg)
        slope = -(
            y * q * q * (q - 2.0 * p * ls_pos)
            + (1.0 - y) * p * p * (2.0 * q * ls_neg - p)
        )
        return both[0:1, :], mean, focal, slope

    denominator, mean, _, slope = logits(note)
    inverse_row[...] = 1.0 / denominator
    grad_row[...] = cw_row[...] * slope
    mean_row[...] = mean

    def finish_grad(total, at):
        wide = lat[at, :].astype(F32)
        return total * factor * (1.0 - wide * wide)

    sister = {"seq": x * 2 + (1 - c)}
    slots = list(range(1, X)) + [0]
    xs = [lax.rem(x + d, X) for d in range(X)]

    def block(ref, k):
        size = ref.shape[0] // S
        return rows(k * size, size, 16)

    def stage1_copy(a, part, first, d):
        k = xs[d] * 2 + (1 - c)
        return remote(
            part.at[block(part, k)], first.at[d],
            st1_sem.at[0, a, d], st1_sem.at[1, a, d], sister,
        )

    def stage1_slot(a, part, first, d):
        copy = stage1_copy(a, part, first, d)
        copy.start()
        sent.append(copy)
        return copy

    def stage2(a, part, first, mid, second, arrived):
        out = []
        for d in range(1, X):
            arrived[d].wait_recv()
            mine = part[block(part, xs[d] * 2 + c), :].astype(F32)
            mid[d - 1] = (mine + first[d].astype(F32)).astype(BF16)
            out.append(
                send(
                    mid.at[d - 1], second.at[d - 1], st2_sem, (a, d - 1),
                    {"seq": xs[d] * 2 + c},
                )
            )
        return out

    def finish(part, first, second, arrived, copies, scale, out):
        arrived[0].wait_recv()
        total = part[block(part, me_s), :].astype(F32) + first[0].astype(F32)
        for d, copy in enumerate(copies):
            copy.wait_recv()
            total = total + second[d].astype(F32)
        out[...] = (total * scale).astype(BF16)

    backward = Chain(own2, in2, pg, up2_sem, down2_sem, finish_grad)

    @pl.loop(0, NU)
    def _(u):
        at = rows(u * unit, unit, unit)
        value_part = w_s[at, :] * inverse_row[...] * grad_row[...]
        score_part = value_part * (v_s[at, :] - mean_row[...])
        vg = value_part.astype(BF16)
        sg = score_part.astype(BF16)
        vg_s[at, :] = vg
        sg_s[at, :] = sg
        own2[at, :] = (nn(sg, queries[...]) + nn(vg, codew[...])).astype(BF16)
        backward.start_unit(u)

    pw[...] = tn(vg_s[...], lat[...]).astype(BF16)
    w_first = {d: stage1_slot(1, pw, w1, d) for d in range(1, X)}
    q_first = {d: stage1_copy(0, pq, q1, d) for d in slots}
    w_first[0] = stage1_copy(1, pw, w1, 0)
    later = [q_first[d] for d in range(1, X)] + [w_first[0], q_first[0]]
    sent.extend(later)

    def start_later():
        for copy in later:
            copy.start()

    def query_part(i):
        width = C // Q_PARTS
        at = pl.ds(i * width, width)
        pq[at, :] = tn(sg_s[:, at], lat[...]).astype(BF16)

    def query_whole():
        pq[...] = tn(sg_s[...], lat[...]).astype(BF16)
        start_later()

    when(negate(inner), query_whole)
    beside = {Q_AT[i]: functools.partial(query_part, i) for i in range(Q_PARTS)}
    beside[Q_AT[-1]] = start_later

    for copy in cw_copies:
        copy.wait_recv()
    cw_total = cw_sum[0]
    for j in range(1, L):
        cw_total = cw_total + cw_sum[j]
    factor = all_codes / cw_total[0:1, 0:1]
    lag = min(LAG_BWD, NC)
    backward.inner_steps(0, MEET_W, lag, beside)
    w_second = stage2(1, pw, w1, ws, w2, w_first)
    backward.inner_steps(MEET_W, MEET_Q, lag, beside)
    q_second = stage2(0, pq, q1, qs, q2, q_first)
    backward.inner_steps(MEET_Q, NC + lag, lag, beside)

    for i in range(S - per_note):
        tot_wait(lax.rem(others + i, S))
    bias_grad = jnp.zeros((1, C), F32)
    for n in range(notes):
        _, _, focal, slope = logits(n)
        bias_grad = bias_grad + cw_row[...] * slope
        loss_s[me_l, n : n + 1, :] = jnp.broadcast_to(
            jnp.sum(focal * cw_row[...], 1, keepdims=True), (1, 128)
        )
    gb_out[...] = (bias_grad * factor)[0, :]
    loss_copies = [
        send(loss_s.at[me_l], loss_s.at[me_l], loss_sem, (d,), {"lab": p})
        for d, p in enumerate(lab_peers)
    ]
    forward.drain()

    early = (NU - 1) * unit
    wide_block = 2 * (D // S)
    by_slot = wide_block % 128 == 0
    if early:
        backward.outer_wait(0, early // chunk)
        pp32[...] = tn(hidden[0:early, :], pg[0:early, :])
    else:
        pp32[...] = jnp.zeros_like(pp32)
    backward.outer_wait(early // chunk, per_unit)
    p_first = {}
    if by_slot:
        for d in slots:
            at = rows(xs[d] * wide_block, wide_block, 128)
            pp[at, :] = (pp32[at, :] + tn(hidden[early:T, at], pg[early:T, :])).astype(BF16)
            p_first[d] = stage1_slot(2, pp, p1, d)
    else:
        pp[...] = (pp32[...] + tn(hidden[early:T, :], pg[early:T, :])).astype(BF16)
        p_first = {d: stage1_slot(2, pp, p1, d) for d in slots}
    p_second = stage2(2, pp, p1, ps, p2, p_first)
    gh_out[...] = nt(pg[...], proj[...]).astype(BF16)
    finish(pw, w1, w2, w_first, w_second, factor, gw_out)
    finish(pq, q1, q2, q_first, q_second, factor, gq_out)
    for copy in loss_copies:
        copy.wait_recv()
    loss = loss_s[0]
    for j in range(1, L):
        loss = loss + loss_s[j]
    loss_out[...] = loss * factor
    backward.drain()
    for copy in tot_sends:
        copy.wait_send()
    finish(pp, p1, p2, p_first, p_second, 1.0, gp_out)
    for copy in sent:
        copy.wait_send()


def finish_kernel(
    loss, gh, gp, gq, gw, gb, loss_out, gh_out, gp_out, gq_out, gw_out, gb_out, loss_s, sem
):
    pairs = [(gh, gh_out), (gq, gq_out), (gw, gw_out), (gp, gp_out), (gb, gb_out), (loss_s, loss_out)]
    copies = [pltpu.make_async_copy(src, dst, sem.at[k]) for k, (src, dst) in enumerate(pairs)]
    for copy in copies[:-1]:
        copy.start()
    for n in range(loss_s.shape[0]):
        loss_s[n] = jnp.max(loss[n : n + 1, :])
    copies[-1].start()
    for copy in copies:
        copy.wait()


def per_device(hidden, proj_weight, queries, code_weight, code_bias, labels, code_counts):
    L = lax.axis_size("lab")
    S = lax.axis_size("seq")
    X = S // 2
    T, D = hidden.shape
    C, E = queries.shape
    notes = labels.shape[0]
    NU = T // fit(T, UNIT)
    NC = T // fit(fit(T, UNIT), CHUNK)
    vmem = pltpu.VMEM
    dma = pltpu.SemaphoreType.DMA
    scratch = [
        vmem((T, D), BF16),
        vmem((D, E), BF16),
        vmem((C, E), BF16),
        vmem((C, E), BF16),
        vmem((C,), F32),
        vmem((notes, C), jnp.int32),
        vmem((1, C), jnp.int32),
        dma((6,)),
        dma((NU,)),
        vmem((T, E), BF16),
        vmem((2, T, E), BF16),
        vmem((T, E), BF16),
        vmem((T, E), BF16),
        vmem((2, T, E), BF16),
        vmem((T, E), BF16),
        vmem((T, C), F32),
        vmem((T, C), F32),
        vmem((S, 2, C), F32),
        vmem((S, 1, C), F32),
        vmem((L, 1, 128), F32),
        vmem((L, notes, 128), F32),
        vmem((1, C), F32),
        vmem((1, C), F32),
        vmem((1, C), F32),
        vmem((1, C), F32),
        vmem((T, C), BF16),
        vmem((T, C), BF16),
        vmem((C, E), BF16),
        vmem((C, E), BF16),
        vmem((D, E), BF16),
        vmem((D, E), F32),
        vmem((X, C // S, E), BF16),
        vmem((X, C // S, E), BF16),
        vmem((X, D // S, E), BF16),
        vmem((X - 1, C // S, E), BF16),
        vmem((X - 1, C // S, E), BF16),
        vmem((X - 1, D // S, E), BF16),
        vmem((X - 1, C // S, E), BF16),
        vmem((X - 1, C // S, E), BF16),
        vmem((X - 1, D // S, E), BF16),
        dma((2, S - 1)),
        dma((2, S)),
        dma((2, L - 1)),
        dma((2, L - 1)),
        dma((3, NC)),
        dma((2, NC)),
        dma((3, NC)),
        dma((2, NC)),
        dma((2, 3, X)),
        dma((2, 3, X - 1)),
    ]
    whole = pl.BlockSpec(memory_space=pltpu.VMEM)
    anywhere = pl.BlockSpec(memory_space=pl.ANY)
    outs = pl.pallas_call(
        functools.partial(kernel, S, L, float(C * L)),
        out_shape=(
            pltpu.VMEM((notes, 128), F32),
            pltpu.VMEM((T, D), BF16),
            pltpu.VMEM((D // S, E), BF16),
            pltpu.VMEM((C // S, E), BF16),
            pltpu.VMEM((C // S, E), BF16),
            pltpu.VMEM((C,), F32),
        ),
        in_specs=[anywhere] * 7,
        scratch_shapes=scratch,
        compiler_params=pltpu.CompilerParams(
            collective_id=0, has_side_effects=True, vmem_limit_bytes=54 * 1024 * 1024
        ),
    )(hidden, proj_weight, queries, code_weight, code_bias, labels, code_counts)
    return pl.pallas_call(
        finish_kernel,
        out_shape=(
            jax.ShapeDtypeStruct((notes,), F32),
            jax.ShapeDtypeStruct((T, D), BF16),
            jax.ShapeDtypeStruct((D // S, E), BF16),
            jax.ShapeDtypeStruct((C // S, E), BF16),
            jax.ShapeDtypeStruct((C // S, E), BF16),
            jax.ShapeDtypeStruct((C,), F32),
        ),
        in_specs=[whole] * 6,
        out_specs=(anywhere,) * 6,
        scratch_shapes=[pltpu.SMEM((notes,), F32), dma((6,))],
    )(*(pltpu.with_memory_space_constraint(out, pltpu.VMEM) for out in outs))


def solution(mesh):
    placed = (
        P(("grp", "seq"), "lab"),
        P("lab", None),
        P("lab", None),
        P("lab", None),
        P("lab"),
        P("grp", "lab"),
        P(("grp", "seq"), "lab"),
    )
    return jax.shard_map(
        per_device,
        mesh=mesh,
        in_specs=placed,
        out_specs=(
            P("grp"),
            P(("grp", "seq"), "lab"),
            P(("grp", "lab", "seq"), None),
            P(("grp", "lab", "seq"), None),
            P(("grp", "lab", "seq"), None),
            P(("grp", "lab")),
        ),
        check_vma=False,
    )
```

```python
import functools
import math

import jax
import jax.numpy as jnp
from jax import lax
from jax.experimental import pallas as pl
from jax.experimental.pallas import tpu as pltpu
from jax.sharding import PartitionSpec as P

balance_beta = 0.9999
MESH = pl.DeviceIdType.MESH
F32 = jnp.float32
BF16 = jnp.bfloat16
CHUNK = 64
UNIT = 256
UNIT_BWD = 128
LAG_FWD = 4
LAG_BWD = 5
MEET_W = 3
MEET_Q = 12
Q_PARTS = 3
Q_AT = (1, 4, 6, 7)


def expm1(x):
    series = jnp.ones_like(x)
    for order in range(10, 1, -1):
        series = 1.0 + x * series * (1.0 / order)
    return jnp.where(jnp.abs(x) < 0.5, x * series, jnp.exp(x) - 1.0)


def nt(a, b):
    return lax.dot_general(a, b, (((1,), (1,)), ((), ())), preferred_element_type=F32)


def tn(a, b):
    return lax.dot_general(a, b, (((0,), (0,)), ((), ())), preferred_element_type=F32)


def nn(a, b):
    return jnp.dot(a, b, preferred_element_type=F32)


def rows(start, size, multiple):
    return pl.ds(pl.multiple_of(start, multiple), size)


def fit(size, want):
    return want if size % want == 0 else size


def both_true(a, b):
    if isinstance(a, bool):
        return b if a else False
    if isinstance(b, bool):
        return a if b else False
    return jnp.logical_and(a, b)


def negate(a):
    return (not a) if isinstance(a, bool) else jnp.logical_not(a)


def when(condition, body):
    if isinstance(condition, bool):
        if condition:
            body()
    else:
        pl.when(condition)(body)


def far_first(count):
    return sorted(range(1, count), key=lambda d: -min(d, count - d))


def kernel(
    S, L, all_codes,
    hidden_h, proj_h, queries_h, codew_h, bias_h, labels_h, counts_h,
    loss_out, gh_out, gp_out, gq_out, gw_out, gb_out,
    hidden, proj, queries, codew, bias, labels, counts, load_sem, hidden_sem, own1, in1, lat, own2, in2, pg,
    w_s, v_s, tot, cnt, cw_sum, loss_s, cw_row, inverse_row, grad_row, mean_row, sg_s, vg_s,
    pq, pw, pp, pp32, q1, w1, p1, qs, ws, ps, q2, w2, p2, p3,
    cnt_sem, tot_sem, cw_sem, loss_sem, up1_sem, down1_sem, up2_sem, down2_sem, st1_sem, st2_sem, straight_sem,
):
    T, D = hidden.shape
    C, E = queries.shape
    notes = labels.shape[0]
    X = S // 2
    per_note = S // notes
    unit = fit(T, UNIT)
    chunk = fit(unit, CHUNK)
    NC = T // chunk
    NU = T // unit
    per_unit = unit // chunk
    half = L // 2
    me_s = lax.axis_index("seq")
    me_l = lax.axis_index("lab")
    x = me_s // 2
    c = lax.rem(me_s, 2)
    lab_peers = [lax.rem(me_l + d, L) for d in range(1, L)]
    seq_peers = [lax.rem(me_s + d, S) for d in range(1, S)]
    side = me_l // half
    inward = me_l + 1 - 2 * side
    outward = lax.rem(me_l - 1 + 2 * side + L, L)
    if L == 2:
        inner, middle = False, True
    else:
        inner = jnp.logical_and(me_l != 0, me_l != L - 1)
        middle = jnp.logical_or(me_l == half - 1, me_l == half)
    across = 1 if L == 2 else jnp.where(middle, 1, 0)
    sent = []
    sent_if = []

    def remote(src, dst, send_sem, recv_sem, device):
        return pltpu.make_async_remote_copy(
            src_ref=src,
            dst_ref=dst,
            send_sem=send_sem,
            recv_sem=recv_sem,
            device_id=device,
            device_id_type=MESH,
        )

    def send(src, dst, sems, index, device):
        copy = remote(src, dst, sems.at[(0,) + index], sems.at[(1,) + index], device)
        copy.start()
        sent.append(copy)
        return copy

    barrier = pltpu.get_barrier_semaphore()
    def greet(peer):
        pl.semaphore_signal(barrier, inc=1, device_id={"lab": peer}, device_id_type=MESH)

    greet(inward)
    when(inner, lambda: greet(outward))
    greetings = S + (0 if L == 2 else jnp.where(inner, 1, 0))

    for peer in seq_peers:
        pl.semaphore_signal(barrier, inc=1, device_id={"seq": peer}, device_id_type=MESH)

    def load(k, src, dst):
        copy = pltpu.make_async_copy(src, dst, load_sem.at[k])
        copy.start()
        return copy

    proj_load = load(0, proj_h, proj)
    hidden_loads = []
    for u in range(NU):
        at = pl.ds(u * unit, unit)
        hidden_loads.append(pltpu.make_async_copy(hidden_h.at[at], hidden.at[at], hidden_sem.at[u]))
        hidden_loads[-1].start()
    counts_load = load(1, counts_h, counts)
    bias_load = load(2, bias_h, bias)
    labels_load = load(3, labels_h, labels)

    def piece(k):
        if isinstance(k, int):
            return pl.ds(k * chunk, chunk)
        return rows(k * chunk, chunk, chunk)

    class Chain:
        def __init__(self, own, arrived, final, up, down, finish):
            self.own, self.arrived, self.final = own, arrived, final
            self.up, self.down, self.finish = up, down, finish

        def up_copy(self, k, slot):
            return remote(
                self.own.at[piece(k)], self.arrived.at[slot, piece(k)],
                self.up.at[2, k], self.up.at[slot, k], {"lab": inward},
            )

        def down_copy(self, k):
            at = self.final.at[piece(k)]
            return remote(at, at, self.down.at[0, k], self.down.at[1, k], {"lab": outward})

        def send_up(self, k):
            self.up_copy(k, across).start()

        def start(self, first, count):
            def body():
                for i in range(count):
                    self.send_up(first + i)

            when(negate(inner), body)

        def sum_with(self, at, slot):
            return self.own[at, :].astype(F32) + self.arrived[slot, at, :].astype(F32)

        def add_up(self, k):
            self.up_copy(k, 0).wait_recv()
            at = piece(k)
            self.own[at, :] = self.sum_with(at, 0).astype(BF16)
            self.send_up(k)

        def settle(self, k, is_middle):
            def meet():
                self.up_copy(k, 1).wait_recv()
                at = piece(k)
                self.final[at, :] = self.finish(self.sum_with(at, 1), at).astype(BF16)

            when(is_middle, meet)
            when(negate(is_middle), lambda: self.down_copy(k).wait_recv())

        def inner_steps(self, first, last, lag, beside={}):
            def body():
                for k in range(first, last):
                    if k < NC:
                        self.add_up(k)
                    if k >= lag:
                        self.settle(k - lag, True if L == 4 else middle)
                        self.down_copy(k - lag).start()
                    if k in beside:
                        beside[k]()

            when(inner, body)

        def outer_wait(self, first, count):
            def body():
                for i in range(count):
                    self.settle(first + i, L == 2)

            when(negate(inner), body)

        def drain(self):
            for k in range(NC):
                self.up_copy(k, 0).wait_send()

            def body():
                for k in range(NC):
                    self.down_copy(k).wait_send()

            when(inner, body)

    def finish_latent(total, at):
        return jnp.tanh(total)

    forward = Chain(own1, in1, lat, up1_sem, down1_sem, finish_latent)

    proj_load.wait()
    for u in range(NU):
        hidden_loads[u].wait()
        at = pl.ds(u * unit, unit)
        own1[at, :] = nn(hidden[at, :], proj[...]).astype(BF16)
        if u == 0:
            pl.semaphore_wait(barrier, greetings)
        forward.start(u * per_unit, per_unit)
    queries_load = load(4, queries_h, queries)
    codew_load = load(5, codew_h, codew)
    counts_load.wait()
    cnt[me_s] = counts[...].astype(F32)
    cnt_copies = [
        send(cnt.at[me_s], cnt.at[me_s], cnt_sem, (d,), {"seq": p})
        for d, p in enumerate(seq_peers)
    ]
    tot[me_s] = jnp.zeros((2, C), F32)
    lag = min(LAG_FWD, NC)
    forward.inner_steps(0, NC + lag, lag)
    for copy in cnt_copies:
        copy.wait_recv()
    occurrences = jnp.ones((1, C), F32)
    for s in range(S):
        occurrences = occurrences + cnt[s]
    class_weight = (1.0 - balance_beta) / -expm1(occurrences * math.log(balance_beta))
    cw_row[...] = class_weight
    cw_sum[me_l] = jnp.broadcast_to(jnp.sum(class_weight, 1, keepdims=True), (1, 128))
    queries_load.wait()
    codew_load.wait()

    @pl.loop(0, NU)
    def _(u):
        forward.outer_wait(u * per_unit, per_unit)
        at = rows(u * unit, unit, unit)
        block = lat[at, :]
        weights = jnp.exp(nt(block, queries[...]))
        values = nt(block, codew[...])
        w_s[at, :] = weights
        v_s[at, :] = values
        tot[me_s, 0:1, :] += jnp.sum(weights, 0, keepdims=True)
        tot[me_s, 1:2, :] += jnp.sum(weights * values, 0, keepdims=True)

    note = me_s // per_note
    sister_at = note * per_note

    def tot_copy(target, index):
        return remote(
            tot.at[me_s], tot.at[me_s], tot_sem.at[0, index], tot_sem.at[1, me_s],
            {"seq": target},
        )

    tot_sends = []
    for i in range(1, per_note):
        target = sister_at + lax.rem(me_s - sister_at + i, per_note)
        tot_sends.append(tot_copy(target, len(tot_sends)))
        tot_sends[-1].start()
    others = lax.rem(sister_at + per_note, S)
    for i in range(S - per_note):
        target = lax.rem(others + i, S)
        tot_sends.append(tot_copy(target, len(tot_sends)))
        tot_sends[-1].start()

    def tot_wait(source):
        remote(
            tot.at[source], tot.at[source], tot_sem.at[0, 0], tot_sem.at[1, source],
            {"seq": seq_peers[0]},
        ).wait_recv()

    cw_copies = [
        send(cw_sum.at[me_l], cw_sum.at[me_l], cw_sem, (d,), {"lab": p})
        for d, p in enumerate(lab_peers)
    ]

    bias_load.wait()
    labels_load.wait()
    for i in range(1, per_note):
        tot_wait(sister_at + lax.rem(me_s - sister_at + i, per_note))

    def logits(n):
        both = tot[n * per_note]
        for i in range(1, per_note):
            both = both + tot[n * per_note + i]
        mean = both[1:2, :] / both[0:1, :]
        logit = mean + bias[...][None, :]
        y = labels[pl.ds(n, 1), :].astype(F32)
        t = jnp.exp(-jnp.abs(logit))
        l1p = jnp.log1p(t)
        big = 1.0 / (1.0 + t)
        small = t / (1.0 + t)
        p = jnp.where(logit >= 0, big, small)
        q = jnp.where(logit >= 0, small, big)
        ls_pos = jnp.minimum(logit, 0.0) - l1p
        ls_neg = jnp.minimum(-logit, 0.0) - l1p
        focal = -(y * q * q * ls_pos + (1.0 - y) * p * p * ls_neg)
        slope = -(
            y * q * q * (q - 2.0 * p * ls_pos)
            + (1.0 - y) * p * p * (2.0 * q * ls_neg - p)
        )
        return both[0:1, :], mean, focal, slope

    denominator, mean, _, slope = logits(note)
    inverse_row[...] = 1.0 / denominator
    grad_row[...] = cw_row[...] * slope
    mean_row[...] = mean

    def finish_grad(total, at):
        wide = lat[at, :].astype(F32)
        return total * factor * (1.0 - wide * wide)

    sister = {"seq": x * 2 + (1 - c)}
    slots = list(range(1, X)) + [0]
    xs = [lax.rem(x + d, X) for d in range(X)]

    def block(ref, k):
        size = ref.shape[0] // S
        return rows(k * size, size, 16)

    def block_from(ref, k, skip):
        size = ref.shape[0] // S
        return rows(k * size + skip, size - skip, 16)

    def stage1_copy(a, part, first, d, skip=0):
        k = xs[d] * 2 + (1 - c)
        return remote(
            part.at[block_from(part, k, skip)], first.at[d, pl.ds(skip, first.shape[1] - skip)],
            st1_sem.at[0, a, d], st1_sem.at[1, a, d], sister,
        )

    def stage1_slot(a, part, first, d, skip=0):
        copy = stage1_copy(a, part, first, d, skip)
        copy.start()
        sent.append(copy)
        return copy

    def stage2(a, part, first, mid, second, arrived, skip=0):
        out = []
        for d in range(1, X):
            arrived[d].wait_recv()
            at = pl.ds(skip, first.shape[1] - skip)
            mine = part[block_from(part, xs[d] * 2 + c, skip), :].astype(F32)
            mid[d - 1, at, :] = (mine + first[d, at, :].astype(F32)).astype(BF16)
            copy = remote(
                mid.at[d - 1, at], second.at[d - 1, at],
                st2_sem.at[0, a, d - 1], st2_sem.at[1, a, d - 1], {"seq": xs[d] * 2 + c},
            )
            copy.start()
            out.append(copy)
        return out

    def finish(part, first, second, arrived, copies, scale, out):
        arrived[0].wait_recv()
        total = part[block(part, me_s), :].astype(F32) + first[0].astype(F32)
        for d, copy in enumerate(copies):
            copy.wait_recv()
            total = total + second[d].astype(F32)
        out[...] = (total * scale).astype(BF16)

    backward = Chain(own2, in2, pg, up2_sem, down2_sem, finish_grad)

    unit_bwd = fit(unit, UNIT_BWD)

    @pl.loop(0, T // unit_bwd)
    def _(u):
        at = rows(u * unit_bwd, unit_bwd, unit_bwd)
        value_part = w_s[at, :] * inverse_row[...] * grad_row[...]
        score_part = value_part * (v_s[at, :] - mean_row[...])
        vg = value_part.astype(BF16)
        sg = score_part.astype(BF16)
        vg_s[at, :] = vg
        sg_s[at, :] = sg
        own2[at, :] = (nn(sg, queries[...]) + nn(vg, codew[...])).astype(BF16)
        backward.start(u * (unit_bwd // chunk), unit_bwd // chunk)

    pw[...] = tn(vg_s[...], lat[...]).astype(BF16)
    w_first = {d: stage1_slot(1, pw, w1, d) for d in range(1, X)}
    q_first = {d: stage1_copy(0, pq, q1, d) for d in slots}
    w_first[0] = stage1_copy(1, pw, w1, 0)
    later = [q_first[d] for d in range(1, X)] + [w_first[0], q_first[0]]
    sent.extend(later)

    def start_later():
        for copy in later:
            copy.start()

    def query_part(i):
        width = C // Q_PARTS
        at = pl.ds(i * width, width)
        pq[at, :] = tn(sg_s[:, at], lat[...]).astype(BF16)

    def query_whole():
        pq[...] = tn(sg_s[...], lat[...]).astype(BF16)
        start_later()

    when(negate(inner), query_whole)
    beside = {Q_AT[i]: functools.partial(query_part, i) for i in range(Q_PARTS)}
    beside[Q_AT[-1]] = start_later

    for copy in cw_copies:
        copy.wait_recv()
    cw_total = cw_sum[0]
    for j in range(1, L):
        cw_total = cw_total + cw_sum[j]
    factor = all_codes / cw_total[0:1, 0:1]
    lag = min(LAG_BWD, NC)
    backward.inner_steps(0, MEET_W, lag, beside)
    w_second = stage2(1, pw, w1, ws, w2, w_first)
    backward.inner_steps(MEET_W, MEET_Q, lag, beside)
    q_second = stage2(0, pq, q1, qs, q2, q_first)
    backward.inner_steps(MEET_Q, NC + lag, lag, beside)

    for i in range(S - per_note):
        tot_wait(lax.rem(others + i, S))
    bias_grad = jnp.zeros((1, C), F32)
    for n in range(notes):
        _, _, focal, slope = logits(n)
        bias_grad = bias_grad + cw_row[...] * slope
        loss_s[me_l, n : n + 1, :] = jnp.broadcast_to(
            jnp.sum(focal * cw_row[...], 1, keepdims=True), (1, 128)
        )
    gb_out[...] = (bias_grad * factor)[0, :]
    loss_copies = [
        send(loss_s.at[me_l], loss_s.at[me_l], loss_sem, (d,), {"lab": p})
        for d, p in enumerate(lab_peers)
    ]
    forward.drain()

    early = (NU - 1) * unit
    wide_block = 2 * (D // S)
    by_slot = wide_block % 128 == 0
    if early:
        backward.outer_wait(0, early // chunk)
        pp32[...] = tn(hidden[0:early, :], pg[0:early, :])
    else:
        pp32[...] = jnp.zeros_like(pp32)
    backward.outer_wait(early // chunk, per_unit)
    size = D // S
    straight = size * 3 // 8 // 16 * 16
    p_first = {}
    p_straight = []
    if not by_slot:
        pp[...] = (pp32[...] + tn(hidden[early:T, :], pg[early:T, :])).astype(BF16)
    for d in slots:
        if by_slot:
            at = rows(xs[d] * wide_block, wide_block, 128)
            pp[at, :] = (pp32[at, :] + tn(hidden[early:T, at], pg[early:T, :])).astype(BF16)
        skip = straight if d else 0
        p_first[d] = stage1_slot(2, pp, p1, d, skip)
        if skip:
            for core in range(2):
                owner = xs[d] * 2 + core
                copy = remote(
                    pp.at[rows(owner * size, skip, 16)], p3.at[d - 1, c],
                    straight_sem.at[0, d - 1, core], straight_sem.at[1, d - 1, c], {"seq": owner},
                )
                copy.start()
                p_straight.append(copy)
    p_second = stage2(2, pp, p1, ps, p2, p_first, straight)
    gh_out[...] = nt(pg[...], proj[...]).astype(BF16)
    finish(pw, w1, w2, w_first, w_second, factor, gw_out)
    finish(pq, q1, q2, q_first, q_second, factor, gq_out)
    for copy in loss_copies:
        copy.wait_recv()
    loss = loss_s[0]
    for j in range(1, L):
        loss = loss + loss_s[j]
    loss_out[...] = loss * factor
    backward.drain()
    for copy in tot_sends + sent + w_second + q_second:
        copy.wait_send()
    own_block = block(pp, me_s)
    p_first[0].wait_recv()
    pp32[0:size, :] = pp[own_block, :].astype(F32) + p1[0].astype(F32)
    if straight:
        for d in range(1, X):
            for core in range(2):
                arriving = remote(
                    pp.at[pl.ds(0, straight)], p3.at[d - 1, core],
                    straight_sem.at[0, d - 1, core], straight_sem.at[1, d - 1, core], sister,
                )
                arriving.wait_recv()
                pp32[0:straight, :] += p3[d - 1, core].astype(F32)
        gp_out[0:straight, :] = pp32[0:straight, :].astype(BF16)
        for copy in p_straight:
            copy.wait_send()
    rest = pp32[straight:size, :]
    for d, copy in enumerate(p_second):
        copy.wait_recv()
        rest = rest + p2[d, straight:size, :].astype(F32)
    gp_out[straight:size, :] = rest.astype(BF16)
    for copy in p_second:
        copy.wait_send()


def finish_kernel(
    loss, gh, gp, gq, gw, gb, loss_out, gh_out, gp_out, gq_out, gw_out, gb_out, loss_s, sem
):
    pairs = [(gh, gh_out), (gq, gq_out), (gw, gw_out), (gp, gp_out), (gb, gb_out), (loss_s, loss_out)]
    copies = [pltpu.make_async_copy(src, dst, sem.at[k]) for k, (src, dst) in enumerate(pairs)]
    for copy in copies[:-1]:
        copy.start()
    for n in range(loss_s.shape[0]):
        loss_s[n] = jnp.max(loss[n : n + 1, :])
    copies[-1].start()
    for copy in copies:
        copy.wait()


def per_device(hidden, proj_weight, queries, code_weight, code_bias, labels, code_counts):
    L = lax.axis_size("lab")
    S = lax.axis_size("seq")
    X = S // 2
    T, D = hidden.shape
    C, E = queries.shape
    notes = labels.shape[0]
    NU = T // fit(T, UNIT)
    NC = T // fit(fit(T, UNIT), CHUNK)
    vmem = pltpu.VMEM
    dma = pltpu.SemaphoreType.DMA
    scratch = [
        vmem((T, D), BF16),
        vmem((D, E), BF16),
        vmem((C, E), BF16),
        vmem((C, E), BF16),
        vmem((C,), F32),
        vmem((notes, C), jnp.int32),
        vmem((1, C), jnp.int32),
        dma((6,)),
        dma((NU,)),
        vmem((T, E), BF16),
        vmem((2, T, E), BF16),
        vmem((T, E), BF16),
        vmem((T, E), BF16),
        vmem((2, T, E), BF16),
        vmem((T, E), BF16),
        vmem((T, C), F32),
        vmem((T, C), F32),
        vmem((S, 2, C), F32),
        vmem((S, 1, C), F32),
        vmem((L, 1, 128), F32),
        vmem((L, notes, 128), F32),
        vmem((1, C), F32),
        vmem((1, C), F32),
        vmem((1, C), F32),
        vmem((1, C), F32),
        vmem((T, C), BF16),
        vmem((T, C), BF16),
        vmem((C, E), BF16),
        vmem((C, E), BF16),
        vmem((D, E), BF16),
        vmem((D, E), F32),
        vmem((X, C // S, E), BF16),
        vmem((X, C // S, E), BF16),
        vmem((X, D // S, E), BF16),
        vmem((X - 1, C // S, E), BF16),
        vmem((X - 1, C // S, E), BF16),
        vmem((X - 1, D // S, E), BF16),
        vmem((X - 1, C // S, E), BF16),
        vmem((X - 1, C // S, E), BF16),
        vmem((X - 1, D // S, E), BF16),
        vmem((X - 1, 2, max(16, D // S * 3 // 8 // 16 * 16), E), BF16),
        dma((2, S - 1)),
        dma((2, S)),
        dma((2, L - 1)),
        dma((2, L - 1)),
        dma((3, NC)),
        dma((2, NC)),
        dma((3, NC)),
        dma((2, NC)),
        dma((2, 3, X)),
        dma((2, 3, X - 1)),
        dma((2, X - 1, 2)),
    ]
    whole = pl.BlockSpec(memory_space=pltpu.VMEM)
    anywhere = pl.BlockSpec(memory_space=pl.ANY)
    outs = pl.pallas_call(
        functools.partial(kernel, S, L, float(C * L)),
        out_shape=(
            pltpu.VMEM((notes, 128), F32),
            pltpu.VMEM((T, D), BF16),
            pltpu.VMEM((D // S, E), BF16),
            pltpu.VMEM((C // S, E), BF16),
            pltpu.VMEM((C // S, E), BF16),
            pltpu.VMEM((C,), F32),
        ),
        in_specs=[anywhere] * 7,
        scratch_shapes=scratch,
        compiler_params=pltpu.CompilerParams(
            collective_id=0, has_side_effects=True, vmem_limit_bytes=54 * 1024 * 1024
        ),
    )(hidden, proj_weight, queries, code_weight, code_bias, labels, code_counts)
    return pl.pallas_call(
        finish_kernel,
        out_shape=(
            jax.ShapeDtypeStruct((notes,), F32),
            jax.ShapeDtypeStruct((T, D), BF16),
            jax.ShapeDtypeStruct((D // S, E), BF16),
            jax.ShapeDtypeStruct((C // S, E), BF16),
            jax.ShapeDtypeStruct((C // S, E), BF16),
            jax.ShapeDtypeStruct((C,), F32),
        ),
        in_specs=[whole] * 6,
        out_specs=(anywhere,) * 6,
        scratch_shapes=[pltpu.SMEM((notes,), F32), dma((6,))],
    )(*(pltpu.with_memory_space_constraint(out, pltpu.VMEM) for out in outs))


def solution(mesh):
    placed = (
        P(("grp", "seq"), "lab"),
        P("lab", None),
        P("lab", None),
        P("lab", None),
        P("lab"),
        P("grp", "lab"),
        P(("grp", "seq"), "lab"),
    )
    return jax.shard_map(
        per_device,
        mesh=mesh,
        in_specs=placed,
        out_specs=(
            P("grp"),
            P(("grp", "seq"), "lab"),
            P(("grp", "lab", "seq"), None),
            P(("grp", "lab", "seq"), None),
            P(("grp", "lab", "seq"), None),
            P(("grp", "lab")),
        ),
        check_vma=False,
    )
```
